32 devices in a mesh: seq: 8 (over z, core), shard: 4 (over y, x).
Axes of the slice: x: 2, y: 2, z: 4, core: 2. Of those that a mesh axis runs over, the one named last changes fastest.
Arguments:
- images: bfloat16 [4, 2304, 1024], P('shard', 'seq'), may hold values from -6 to 6
- norm1_scale: bfloat16 [2, 1024], P(None, 'shard'), may hold values from 0.5 to 1.5
- norm1_shift: bfloat16 [2, 1024], P(None, 'shard'), may hold values from -1.5 to 1.5
- qkv_weight: bfloat16 [2, 1024, 3072], P(None, 'shard'), may hold values from -0.25 to 0.25
- qv_bias: bfloat16 [2, 2048], P(None, 'shard'), may hold values from -1.5 to 1.5
- out_weight: bfloat16 [2, 1024, 1024], P(None, 'shard'), may hold values from -0.75 to 0.75
- out_bias: bfloat16 [2, 1024], P(None, 'shard'), may hold values from -1.5 to 1.5
- norm2_scale: bfloat16 [2, 1024], P(None, 'shard'), may hold values from 0.5 to 1.5
- norm2_shift: bfloat16 [2, 1024], P(None, 'shard'), may hold values from -1.5 to 1.5
- up_weight: bfloat16 [2, 1024, 4096], P(None, 'shard'), may hold values from -0.1875 to 0.1875
- up_bias: bfloat16 [2, 4096], P(None, 'shard'), may hold values from -2.5 to 2.5
- down_weight: bfloat16 [2, 4096, 1024], P(None, 'shard'), may hold values from -0.125 to 0.125
- down_bias: bfloat16 [2, 1024], P(None, 'shard'), may hold values from -1.5 to 1.5
- cotangent: bfloat16 [4, 2304, 1024], P('shard', 'seq'), may hold values from -6 to 6
Outputs:
- outputs: bfloat16 [4, 2304, 1024], P('shard', 'seq')
- input_grad: float32 [4, 2304, 1024], P('shard', 'seq')
- grad_norm1_scale: float32 [2, 1024], P(None, 'shard')
- grad_norm1_shift: float32 [2, 1024], P(None, 'shard')
- grad_qkv_weight: float32 [2, 1024, 3072], P(None, 'shard')
- grad_qv_bias: float32 [2, 2048], P(None, 'shard')
- grad_out_weight: float32 [2, 1024, 1024], P(None, 'shard')
- grad_out_bias: float32 [2, 1024], P(None, 'shard')
- grad_norm2_scale: float32 [2, 1024], P(None, 'shard')
- grad_norm2_shift: float32 [2, 1024], P(None, 'shard')
- grad_up_weight: float32 [2, 1024, 4096], P(None, 'shard')
- grad_up_bias: float32 [2, 4096], P(None, 'shard')
- grad_down_weight: float32 [2, 4096, 1024], P(None, 'shard')
- grad_down_bias: float32 [2, 1024], P(None, 'shard')
The draws below stay inside these ranges and needn't reach their ends.
All inputs are finite; a program needn't handle non-finite values.
Results may differ from the reference program's by a relative error of at most 0.015.
Values may be sent and summed in bfloat16 or wider, within the bound.
No kernel may reach another device: no remote copies, remote signals or barrier semaphores. Data moves between devices by JAX's collectives and lax.ppermute only.
A program may use at most 320 MiB of HBM per device.

```python
import jax
import jax.numpy as jnp
from jax import lax

D = 1024
H = 16
HD = 64
FF = 4096
LEN = 2304
LAYERS = 2
IMAGES = 4


def levels(stream_key, shape, shards, low, top_value):
    factor_of, own = 1.0, jax.random.fold_in(stream_key, 6)
    for axis_at, shards_of in shards:
        heights = jnp.exp(jax.random.uniform(jax.random.fold_in(own, axis_at), (shards_of,), jnp.float32, low / len(shards), top_value / len(shards)))
        factor_of = factor_of * jnp.repeat(heights, shape[axis_at] // shards_of).reshape([-1 if axis == axis_at else 1 for axis in range(len(shape))])
    return factor_of


def normal_values(key, extent, deviation, bound, cuts=(), dtype=jnp.bfloat16):
    entries = jax.random.normal(key, extent, jnp.float32) * deviation
    if len(cuts) > 0:
        entries = levels(key, extent, cuts, -0.22, 0.18) * entries
    return jnp.clip(entries, min=-bound, max=bound).astype(dtype)


def setup_inputs(seed: int = 0) -> dict:
    keys = jax.random.split(jax.random.key(seed), 15)
    images = normal_values(keys[0], (IMAGES, LEN, D), 1.0, 6.0, ((0, 4), (1, 8)))
    norm1_scale = jnp.clip(0.5 + 1.0 * jax.random.uniform(keys[1], (LAYERS, D), jnp.float32) ** levels(keys[1], (LAYERS, D), ((1, 4),), -0.2, 0.2), 0.5, 1.5).astype(jnp.bfloat16)
    norm1_shift = normal_values(keys[2], (LAYERS, D), 0.3, 1.5, ((1, 4),))
    qkv_weight = normal_values(keys[3], (LAYERS, D, 3 * D), (D // 2) ** -0.5, 0.25, ((1, 4),))
    qv_bias = normal_values(keys[4], (LAYERS, 2 * D), 0.3, 1.5, ((1, 4),))
    out_weight = normal_values(keys[5], (LAYERS, D, D), (D // 16) ** -0.5, 0.75, ((1, 4),))
    out_bias = normal_values(keys[6], (LAYERS, D), 0.3, 1.5, ((1, 4),))
    norm2_scale = jnp.clip(0.5 + 1.0 * jax.random.uniform(keys[7], (LAYERS, D), jnp.float32) ** levels(keys[7], (LAYERS, D), ((1, 4),), -0.2, 0.2), 0.5, 1.5).astype(jnp.bfloat16)
    norm2_shift = normal_values(keys[8], (LAYERS, D), 0.3, 1.5, ((1, 4),))
    up_weight = normal_values(keys[9], (LAYERS, D, FF), D ** -0.5, 0.1875, ((1, 4),))
    up_bias = normal_values(keys[10], (LAYERS, FF), 0.5, 2.5, ((1, 4),))
    down_weight = normal_values(keys[11], (LAYERS, FF, D), (FF // 2) ** -0.5, 0.125, ((1, 4),))
    down_bias = normal_values(keys[12], (LAYERS, D), 0.3, 1.5, ((1, 4),))
    cotangent = normal_values(keys[13], (IMAGES, LEN, D), 1.0, 6.0, ((0, 4), (1, 8)))
    return dict(images=images, norm1_scale=norm1_scale, norm1_shift=norm1_shift, qkv_weight=qkv_weight, qv_bias=qv_bias, out_weight=out_weight, out_bias=out_bias, norm2_scale=norm2_scale, norm2_shift=norm2_shift, up_weight=up_weight, up_bias=up_bias, down_weight=down_weight, down_bias=down_bias, cotangent=cotangent)


@jax.custom_vjp
def low(v):
    return lax.optimization_barrier(v.astype(jnp.bfloat16)).astype(jnp.float32)

@jax.custom_vjp
def low_back(v):
    return v

def low_keep(v):
    return (low(v), None)

def low_pass(kept, grad):
    return (grad,)

def back_keep(v):
    return (v, None)

def back_low(kept, grad):
    return (low(grad),)
low.defvjp(low_keep, low_pass)
low_back.defvjp(back_keep, back_low)

def matmul_high(left, right):
    return jnp.dot(left, right, precision=lax.Precision.HIGHEST)

def norm_rows(stream, scales, offset):
    average = lax.optimization_barrier(jnp.mean(stream, axis=-1, keepdims=True))
    centered = stream - average
    variance = lax.optimization_barrier(jnp.mean(centered * centered, axis=-1, keepdims=True))
    return centered * lax.rsqrt(variance + 1e-06) * scales + offset

def attend_image(query_heads, key_heads, value_heads):
    query_rows = 768 if LEN % 768 == 0 else LEN
    score_scale = HD ** (-0.5)
    query_blocks = query_heads.reshape(LEN // query_rows, query_rows, H, HD)

    def one_block(query_block):
        scores = jnp.einsum('qhd,khd->hqk', query_block, key_heads, precision=lax.Precision.HIGHEST) * score_scale
        scores = low_back(scores)
        probability = jax.nn.softmax(scores, axis=-1)
        return jnp.einsum('hqk,khd->qhd', low(probability), value_heads, precision=lax.Precision.HIGHEST)
    return lax.map(jax.checkpoint(one_block), query_blocks).reshape(LEN, H * HD)

def layer_forward(stream, weights):
    scale_one, shift_one, qkv_full, qv_full, out_full, out_shift, scale_two, shift_two, up_full, up_shift, down_full, down_shift = weights
    normed_one = low(norm_rows(stream, scale_one, shift_one))
    bias_full = jnp.concatenate([qv_full[:D], jnp.zeros((D,), jnp.float32), qv_full[D:]])
    projected = low_back(low(matmul_high(normed_one, qkv_full) + bias_full))
    head_view = projected.reshape(LEN, 3, H, HD)
    attended = attend_image(head_view[:, 0], head_view[:, 1], head_view[:, 2])
    attended = low_back(low(attended))
    branch_out = low_back(matmul_high(attended, out_full) + out_shift)
    middle = stream + branch_out
    normed_two = low(norm_rows(middle, scale_two, shift_two))
    pre_act = low_back(matmul_high(normed_two, up_full) + up_shift)
    hidden = low(jax.nn.gelu(pre_act, approximate=False))
    mlp_out = low_back(matmul_high(hidden, down_full) + down_shift)
    return middle + mlp_out

def reference(images, norm1_scale, norm1_shift, qkv_weight, qv_bias, out_weight, out_bias, norm2_scale, norm2_shift, up_weight, up_bias, down_weight, down_bias, cotangent):
    params = tuple((member.astype(jnp.float32) for member in (norm1_scale, norm1_shift, qkv_weight, qv_bias, out_weight, out_bias, norm2_scale, norm2_shift, up_weight, up_bias, down_weight, down_bias)))
    inputs = images.astype(jnp.float32)

    def forward(inputs, params):

        def one_image(tokens):
            for layer_index in range(LAYERS):
                tokens = layer_forward(tokens, tuple((member[layer_index] for member in params)))
            return tokens
        return lax.map(jax.checkpoint(one_image), inputs)
    results, pullback = jax.vjp(forward, inputs, params)
    input_grad, param_grads = pullback(cotangent.astype(jnp.float32))
    return (results.astype(jnp.bfloat16), input_grad, param_grads[0], param_grads[1], param_grads[2], param_grads[3], param_grads[4], param_grads[5], param_grads[6], param_grads[7], param_grads[8], param_grads[9], param_grads[10], param_grads[11])
```

```python
from functools import partial

import jax
import jax.numpy as jnp
from jax import lax
from jax.experimental import pallas as pl
from jax.experimental.pallas import tpu as pltpu
from jax.sharding import Mesh
from jax.sharding import PartitionSpec as P

HD = 64
SCALE = HD ** (-0.5)
F32 = jnp.float32
BF16 = jnp.bfloat16
VMEM_BYTES = 56 * 1024 * 1024


def matmul(left, right):
    return jnp.dot(left, right, preferred_element_type=F32)


def outer_sum(left, right):
    return lax.dot_general(left, right, (((0,), (0,)), ((), ())), preferred_element_type=F32)


def times_transposed(left, right):
    return lax.dot_general(left, right, (((1,), (1,)), ((), ())), preferred_element_type=F32)


def norm_forward(stream, scales, offset):
    average = jnp.mean(stream, axis=-1, keepdims=True)
    centered = stream - average
    variance = jnp.mean(centered * centered, axis=-1, keepdims=True)
    inverse = lax.rsqrt(variance + 1e-06)
    return (centered * inverse * scales + offset).astype(BF16), average, inverse


def norm_backward(stream, average, inverse, scales, upstream):
    unit_rows = (stream - average) * inverse
    grad_scale = jnp.sum(upstream * unit_rows, axis=0)
    grad_shift = jnp.sum(upstream, axis=0)
    scaled_grad = upstream * scales
    stream_grad = inverse * (
        scaled_grad
        - jnp.mean(scaled_grad, axis=-1, keepdims=True)
        - unit_rows * jnp.mean(scaled_grad * unit_rows, axis=-1, keepdims=True)
    )
    return stream_grad, grad_scale, grad_shift


def block_rows(tokens):
    for rows in (288, 192, 144, 96, 48, 16):
        if tokens % rows == 0:
            return rows
    return tokens


def lane_head(width):
    return lax.broadcasted_iota(jnp.int32, (1, width), 1) // HD


def attend_kernel(q_ref, k_ref, v_ref, o_ref, lse_ref, ext_ref):
    width = q_ref.shape[-1]
    seq = ext_ref.shape[0]

    @pl.when((pl.program_id(0) == 0) & (pl.program_id(1) == 0))
    def _():
        ext_ref[:, :width] = v_ref[:, 0].reshape(seq, width)
        ext_ref[:, width:] = jnp.ones((seq, ext_ref.shape[1] - width), BF16)

    queries = q_ref[0, 0] * SCALE
    keys = k_ref[:, 0].reshape(seq, width)
    lane = lane_head(width)
    mixed = jnp.zeros(queries.shape, F32)
    logs = jnp.zeros(queries.shape, F32)
    for head in range(width // HD):
        own = lane == head
        scores = times_transposed(jnp.where(own, queries, 0).astype(BF16), keys)
        row_max = jnp.max(scores, axis=1, keepdims=True)
        weight = jnp.exp(scores - row_max).astype(BF16)
        total = matmul(weight, ext_ref[...])
        row_total = total[:, width : 2 * width]
        mixed = jnp.where(own, total[:, :width] / row_total, mixed)
        logs = jnp.where(own, row_max + jnp.log(row_total), logs)
    o_ref[0] = mixed.astype(BF16)
    lse_ref[0] = logs


def attend(packed):
    parts, _, tokens, width = packed.shape
    rows = block_rows(tokens)
    return pl.pallas_call(
        attend_kernel,
        name="attend",
        grid=(parts, tokens // rows),
        in_specs=[
            pl.BlockSpec((1, 1, rows, width), lambda i, j: (i, 0, j, 0)),
            pl.BlockSpec((parts, 1, tokens, width), lambda i, j: (0, 1, 0, 0)),
            pl.BlockSpec((parts, 1, tokens, width), lambda i, j: (0, 2, 0, 0)),
        ],
        out_specs=[
            pl.BlockSpec((1, rows, width), lambda i, j: (i, j, 0)),
            pl.BlockSpec((1, rows, width), lambda i, j: (i, j, 0)),
        ],
        out_shape=[
            jax.ShapeDtypeStruct((parts, tokens, width), BF16),
            jax.ShapeDtypeStruct((parts, tokens, width), F32),
        ],
        scratch_shapes=[pltpu.VMEM((parts * tokens, 2 * width), BF16)],
        compiler_params=pltpu.CompilerParams(vmem_limit_bytes=VMEM_BYTES),
    )(packed, packed, packed)


def attend_back_kernel(q_ref, k_ref, v_ref, o_ref, g_ref, lse_ref, out_ref, dk_ref, dv_ref):
    part, block = pl.program_id(0), pl.program_id(1)
    parts, tokens = k_ref.shape[0], k_ref.shape[2]
    rows, width = q_ref.shape[2], q_ref.shape[3]
    seq = parts * tokens

    @pl.when((part == 0) & (block == 0))
    def _():
        dk_ref[...] = jnp.zeros_like(dk_ref)
        dv_ref[...] = jnp.zeros_like(dv_ref)

    queries = q_ref[0, 0] * SCALE
    grads = g_ref[0]
    keys = k_ref[:, 0].reshape(seq, width)
    values = v_ref[:, 0].reshape(seq, width)
    product = grads.astype(F32) * o_ref[0].astype(F32)
    logs = lse_ref[0]
    query_rows = queries.T
    grad_rows = grads.T
    lane = lane_head(width)
    dquery = jnp.zeros((rows, width), F32)
    for head in range(width // HD):
        own = lane == head
        span = slice(head * HD, (head + 1) * HD)
        scores = times_transposed(jnp.where(own, queries, 0).astype(BF16), keys)
        weight = jnp.exp(scores - logs[:, head * HD : head * HD + 1])
        inner = jnp.sum(jnp.where(own, product, 0.0), axis=1, keepdims=True)
        weight_grad = times_transposed(jnp.where(own, grads, 0).astype(BF16), values)
        score_grad = (weight * (weight_grad - inner)).astype(BF16)
        dv_ref[span, :] += matmul(grad_rows[span], weight.astype(BF16))
        dk_ref[span, :] += matmul(query_rows[span], score_grad)
        dquery = jnp.where(own, matmul(score_grad, keys), dquery)
    out_ref[part, 0, pl.ds(pl.multiple_of(block * rows, rows), rows), :] = (dquery * SCALE).astype(BF16)

    @pl.when((part == parts - 1) & (block == pl.num_programs(1) - 1))
    def _():
        out_ref[:, 1] = dk_ref[...].T.astype(BF16).reshape(parts, tokens, width)
        out_ref[:, 2] = dv_ref[...].T.astype(BF16).reshape(parts, tokens, width)


def attend_back(packed, mixed, grads, logs):
    parts, _, tokens, width = packed.shape
    rows = block_rows(tokens)
    own = pl.BlockSpec((1, rows, width), lambda i, j: (i, j, 0))
    return pl.pallas_call(
        attend_back_kernel,
        name="attend_back",
        grid=(parts, tokens // rows),
        in_specs=[
            pl.BlockSpec((1, 1, rows, width), lambda i, j: (i, 0, j, 0)),
            pl.BlockSpec((parts, 1, tokens, width), lambda i, j: (0, 1, 0, 0)),
            pl.BlockSpec((parts, 1, tokens, width), lambda i, j: (0, 2, 0, 0)),
            own,
            own,
            own,
        ],
        out_specs=pl.BlockSpec((parts, 3, tokens, width), lambda i, j: (0, 0, 0, 0)),
        out_shape=jax.ShapeDtypeStruct((parts, 3, tokens, width), BF16),
        scratch_shapes=[
            pltpu.VMEM((width, parts * tokens), F32),
            pltpu.VMEM((width, parts * tokens), F32),
        ],
        compiler_params=pltpu.CompilerParams(vmem_limit_bytes=VMEM_BYTES),
    )(packed, packed, packed, mixed, grads, logs)


def xor_order(pieces, index):
    count = pieces.shape[0]
    bit = 1
    while bit < count:
        split = pieces.reshape((count // (2 * bit), 2, bit) + pieces.shape[1:])
        pieces = jnp.where((index & bit) != 0, split[:, ::-1], split).reshape(pieces.shape)
        bit *= 2
    return pieces


def exchange(pieces):
    count = pieces.shape[0]
    return jnp.stack(
        [pieces[0]]
        + [lax.ppermute(pieces[k], "z", [(i, i ^ k) for i in range(count)]) for k in range(1, count)]
    )


def swap(value):
    return lax.ppermute(value, "c", [(0, 1), (1, 0)])


def with_partner(rows):
    return jnp.concatenate([rows, swap(rows)], axis=0)


def sum_with_partner(partial_rows):
    half = partial_rows.shape[0] // 2
    return partial_rows[:half] + swap(partial_rows[half:])


def add_rounded(left, right):
    return (left.astype(F32) + right.astype(F32)).astype(BF16)


def sum_over_z(values, index):
    count = lax.axis_size("z")
    bit = 1
    while bit < count:
        pairs = [(i, i ^ bit) for i in range(count)]
        upper = ((index & bit) != 0).astype(jnp.int32)
        halves = values.reshape((2, values.shape[0] // 2) + values.shape[1:])
        sent = lax.dynamic_index_in_dim(halves, 1 - upper, 0, keepdims=False)
        kept = lax.dynamic_index_in_dim(halves, upper, 0, keepdims=False)
        values = add_rounded(kept, lax.ppermute(sent, "z", pairs))
        bit *= 2
    while bit > 1:
        bit //= 2
        pairs = [(i, i ^ bit) for i in range(count)]
        upper = (index & bit) != 0
        other = lax.ppermute(values, "z", pairs)
        values = jnp.concatenate([jnp.where(upper, other, values), jnp.where(upper, values, other)], axis=0)
    return values


def gelu_parts(pre_act):
    cdf = 0.5 * (1.0 + lax.erf(pre_act * (0.5**0.5)))
    density = jnp.exp(-0.5 * pre_act * pre_act) * 0.3989422804014327
    return (pre_act * cdf).astype(BF16), (cdf + pre_act * density).astype(BF16)


def body(
    images,
    norm1_scale,
    norm1_shift,
    qkv_weight,
    qv_bias,
    out_weight,
    out_bias,
    norm2_scale,
    norm2_shift,
    up_weight,
    up_bias,
    down_weight,
    down_bias,
    cotangent,
):
    image_count, local_len, width = images.shape
    z_count = lax.axis_size("z")
    shards = lax.axis_size("shard")
    z_index, c_index, s_index = lax.axis_index("z"), lax.axis_index("c"), lax.axis_index("shard")
    layers = norm1_scale.shape[0]
    hidden_units = up_bias.shape[1] * shards
    half_width = width // 2
    group = half_width // z_count
    tokens = 2 * local_len

    def my_half(values, axis):
        return lax.dynamic_index_in_dim(values, c_index, axis, keepdims=False)

    def gather(values):
        return lax.all_gather(values, "shard", axis=0, tiled=True)

    vectors = (norm1_scale, norm1_shift, out_bias, norm2_scale, norm2_shift, down_bias, qv_bias, up_bias)
    sizes = [member.shape[1] for member in vectors]
    offsets = [sum(sizes[:place]) for place in range(len(sizes) + 1)]
    small = lax.all_gather(jnp.concatenate(vectors, axis=1), "shard", axis=0)

    def full_vector(layer, place):
        return small[:, layer, offsets[place] : offsets[place + 1]].reshape(-1).astype(F32)

    weights = []
    for layer in range(layers):
        qkv_part = my_half(qkv_weight[layer].reshape(-1, 3, shards, 2, half_width // shards), 3)
        qkv_part = jnp.swapaxes(qkv_part.reshape(-1, 3, z_count, group), 1, 2)
        up_part = my_half(up_weight[layer].reshape(-1, shards, 2, hidden_units // 2 // shards), 2)
        weights.append(
            (
                gather(qkv_part.reshape(-1, 3 * half_width)),
                gather(my_half(out_weight[layer].reshape(2, -1, width), 0)),
                gather(up_part.reshape(-1, hidden_units // 2)),
                gather(my_half(down_weight[layer].reshape(2, -1, width), 0)),
            )
        )

    stream = images.astype(F32).reshape(-1, width)
    saved = []
    for layer in range(layers):
        qkv_full, out_full, up_full, down_full = weights[layer]
        scale_one, shift_one, out_shift, scale_two, shift_two, down_shift, qv_full, up_all = [
            full_vector(layer, place) for place in range(8)
        ]
        qv_halves = my_half(qv_full.reshape(2, shards, 2, half_width // shards), 2).reshape(2, z_count, group)
        qkv_shift = jnp.stack([qv_halves[0], jnp.zeros_like(qv_halves[0]), qv_halves[1]], axis=1).reshape(-1)
        up_shift = my_half(up_all.reshape(shards, 2, -1), 1).reshape(-1)

        normed_own, average_one, inverse_one = norm_forward(stream, scale_one, shift_one)
        normed_one = with_partner(normed_own)
        projected = (matmul(normed_one, qkv_full) + qkv_shift).astype(BF16)
        pieces = projected.reshape(tokens, z_count, 3, group).transpose(1, 2, 0, 3)
        packed = exchange(xor_order(pieces, z_index))
        mixed, logs = attend(packed)
        attended = xor_order(exchange(mixed), z_index).transpose(1, 0, 2).reshape(tokens, half_width)
        middle = stream + sum_with_partner(matmul(attended, out_full)) + out_shift
        two_own, average_two, inverse_two = norm_forward(middle, scale_two, shift_two)
        normed_two = with_partner(two_own)
        pre_act = matmul(normed_two, up_full) + up_shift
        hidden, slope = gelu_parts(pre_act)
        saved.append(
            (
                stream,
                average_one,
                inverse_one,
                normed_one,
                packed,
                mixed,
                logs,
                attended,
                middle,
                average_two,
                inverse_two,
                normed_two,
                hidden,
                slope,
                scale_one,
                scale_two,
            )
        )
        stream = middle + sum_with_partner(matmul(hidden, down_full)) + down_shift
    results = stream.astype(BF16).reshape(image_count, local_len, width)

    def reduce_weight(gradient):
        piece = lax.psum_scatter(gradient.astype(BF16), "shard", scatter_dimension=0, tiled=True)
        piece = sum_over_z(piece, z_index)
        other = swap(piece)
        first = jnp.where(c_index == 0, piece, other)
        second = jnp.where(c_index == 0, other, piece)
        return first, second

    grad_stream = cotangent.astype(F32).reshape(-1, width)
    weight_grads = [None] * layers
    small_grads = [None] * layers
    for layer in reversed(range(layers)):
        (
            stream_in,
            average_one,
            inverse_one,
            normed_one,
            packed,
            mixed,
            logs,
            attended,
            middle,
            average_two,
            inverse_two,
            normed_two,
            hidden,
            slope,
            scale_one,
            scale_two,
        ) = saved[layer]
        qkv_full, out_full, up_full, down_full = weights[layer]
        branch_own = grad_stream.astype(BF16)
        branch_grad = with_partner(branch_own)
        grad_down_b = jnp.sum(branch_own.astype(F32), axis=0)
        pre_grad = (times_transposed(branch_grad, down_full) * slope.astype(F32)).astype(BF16)
        two_grad = sum_with_partner(times_transposed(pre_grad, up_full))
        grad_down = reduce_weight(outer_sum(hidden, branch_grad))
        grad_up = reduce_weight(outer_sum(normed_two, pre_grad))
        grad_up_b = jnp.sum(pre_grad.astype(F32), axis=0)
        middle_back, grad_scale_two, grad_shift_two = norm_backward(
            middle, average_two, inverse_two, scale_two, two_grad
        )
        middle_grad = grad_stream + middle_back
        out_own = middle_grad.astype(BF16)
        out_grad = with_partner(out_own)
        grad_out_b = jnp.sum(out_own.astype(F32), axis=0)
        attended_grad = times_transposed(out_grad, out_full).astype(BF16)
        grad_pieces = attended_grad.reshape(tokens, z_count, group).transpose(1, 0, 2)
        head_grad = exchange(xor_order(grad_pieces, z_index))
        grad_out = reduce_weight(outer_sum(attended, out_grad))
        heads_back = attend_back(packed, mixed, head_grad, logs)
        projected_grad = xor_order(exchange(heads_back), z_index).transpose(2, 0, 1, 3)
        projected_grad = projected_grad.reshape(tokens, 3 * half_width)
        one_grad = sum_with_partner(times_transposed(projected_grad, qkv_full))
        grad_qkv = reduce_weight(outer_sum(normed_one, projected_grad))
        column_sums = jnp.sum(projected_grad.astype(F32), axis=0).reshape(z_count, 3, group)
        grad_qv_b = jnp.stack([column_sums[:, 0], column_sums[:, 2]])
        stream_back, grad_scale_one, grad_shift_one = norm_backward(
            stream_in, average_one, inverse_one, scale_one, one_grad
        )
        grad_stream = middle_grad + stream_back

        def spread(values, lead):
            values = values.reshape(lead, shards, 1, -1)
            nothing = jnp.zeros_like(values)
            halves = jnp.concatenate(
                [
                    jnp.where(c_index == 0, values, nothing),
                    jnp.where(c_index == 0, nothing, values),
                ],
                axis=2,
            )
            return halves.reshape(shards, -1)

        small_grads[layer] = jnp.concatenate(
            [
                member.reshape(shards, -1)
                for member in (
                    grad_scale_one,
                    grad_shift_one,
                    grad_out_b,
                    grad_scale_two,
                    grad_shift_two,
                    grad_down_b,
                    spread(grad_qv_b, 2),
                    spread(grad_up_b, 1),
                )
            ],
            axis=1,
        )
        weight_grads[layer] = (grad_qkv, grad_out, grad_up, grad_down)

    small_sums = lax.psum(jnp.stack(small_grads, axis=1), ("z", "c", "shard"))
    small_sums = lax.dynamic_index_in_dim(small_sums, s_index, 0, keepdims=False)
    vector_grads = [small_sums[:, offsets[place] : offsets[place + 1]] for place in range(8)]

    def join_qkv(pair):
        halves = jnp.stack([part.reshape(-1, z_count, 3, group) for part in pair], axis=0)
        halves = halves.transpose(1, 3, 0, 2, 4).reshape(-1, 3, 2, shards, half_width // shards)
        return jnp.swapaxes(halves, 2, 3).reshape(-1, 3 * width).astype(F32)

    def join_up(pair):
        halves = jnp.stack([part.reshape(-1, shards, hidden_units // 2 // shards) for part in pair], axis=2)
        return halves.reshape(-1, hidden_units).astype(F32)

    def join_rows(pair):
        return jnp.concatenate(pair, axis=0).astype(F32)

    grad_qkv = jnp.stack([join_qkv(member[0]) for member in weight_grads])
    grad_out = jnp.stack([join_rows(member[1]) for member in weight_grads])
    grad_up = jnp.stack([join_up(member[2]) for member in weight_grads])
    grad_down = jnp.stack([join_rows(member[3]) for member in weight_grads])
    input_grad = grad_stream.reshape(image_count, local_len, width)
    return (
        results,
        input_grad,
        vector_grads[0],
        vector_grads[1],
        grad_qkv,
        vector_grads[6],
        grad_out,
        vector_grads[2],
        vector_grads[3],
        vector_grads[4],
        grad_up,
        vector_grads[7],
        grad_down,
        vector_grads[5],
    )


def solution(mesh):
    seq, shards = mesh.devices.shape
    cores = Mesh(mesh.devices.reshape(seq // 2, 2, shards), ("z", "c", "shard"))
    rows = P("shard", ("z", "c"), None)
    vector = P(None, "shard")
    matrix = P(None, "shard", None)
    parameters = (
        vector,
        vector,
        matrix,
        vector,
        matrix,
        vector,
        vector,
        vector,
        matrix,
        vector,
        matrix,
        vector,
    )
    return jax.shard_map(
        body,
        mesh=cores,
        in_specs=(rows,) + parameters + (rows,),
        out_specs=(rows, rows) + parameters,
        check_vma=False,
    )
```

```python
from functools import partial

import jax
import jax.numpy as jnp
from jax import lax
from jax.experimental import pallas as pl
from jax.experimental.pallas import tpu as pltpu
from jax.sharding import Mesh
from jax.sharding import PartitionSpec as P

HD = 64
SCALE = HD ** (-0.5)
F32 = jnp.float32
BF16 = jnp.bfloat16
VMEM_BYTES = 56 * 1024 * 1024


def matmul(left, right):
    return jnp.dot(left, right, preferred_element_type=F32)


def outer_sum(left, right):
    return lax.dot_general(left, right, (((0,), (0,)), ((), ())), preferred_element_type=F32)


def times_transposed(left, right):
    return lax.dot_general(left, right, (((1,), (1,)), ((), ())), preferred_element_type=F32)


def norm_forward(stream, scales, offset):
    average = jnp.mean(stream, axis=-1, keepdims=True)
    centered = stream - average
    variance = jnp.mean(centered * centered, axis=-1, keepdims=True)
    inverse = lax.rsqrt(variance + 1e-06)
    return (centered * inverse * scales + offset).astype(BF16), average, inverse


def norm_backward(stream, average, inverse, scales, upstream):
    unit_rows = (stream - average) * inverse
    grad_scale = jnp.sum(upstream * unit_rows, axis=0)
    grad_shift = jnp.sum(upstream, axis=0)
    scaled_grad = upstream * scales
    stream_grad = inverse * (
        scaled_grad
        - jnp.mean(scaled_grad, axis=-1, keepdims=True)
        - unit_rows * jnp.mean(scaled_grad * unit_rows, axis=-1, keepdims=True)
    )
    return stream_grad, grad_scale, grad_shift


def block_rows(tokens):
    for rows in (288, 192, 144, 96, 48, 16):
        if tokens % rows == 0:
            return rows
    return tokens


def lane_head(width):
    return lax.broadcasted_iota(jnp.int32, (1, width), 1) // HD


def attend_kernel(q_ref, k_ref, v_ref, o_ref, lse_ref, ext_ref):
    width = q_ref.shape[-1]
    seq = ext_ref.shape[0]

    @pl.when((pl.program_id(0) == 0) & (pl.program_id(1) == 0))
    def _():
        ext_ref[:, :width] = v_ref[:, 0].reshape(seq, width)
        ext_ref[:, width:] = jnp.ones((seq, ext_ref.shape[1] - width), BF16)

    queries = q_ref[0, 0] * SCALE
    keys = k_ref[:, 0].reshape(seq, width)
    lane = lane_head(width)
    mixed = jnp.zeros(queries.shape, F32)
    logs = jnp.zeros(queries.shape, F32)
    for head in range(width // HD):
        own = lane == head
        scores = times_transposed(jnp.where(own, queries, 0).astype(BF16), keys)
        row_max = jnp.max(scores, axis=1, keepdims=True)
        weight = jnp.exp(scores - row_max).astype(BF16)
        total = matmul(weight, ext_ref[...])
        row_total = total[:, width : 2 * width]
        mixed = jnp.where(own, total[:, :width] / row_total, mixed)
        logs = jnp.where(own, row_max + jnp.log(row_total), logs)
    o_ref[0] = mixed.astype(BF16)
    lse_ref[0] = logs


def attend(packed):
    parts, _, tokens, width = packed.shape
    rows = block_rows(tokens)
    return pl.pallas_call(
        attend_kernel,
        name="attend",
        grid=(parts, tokens // rows),
        in_specs=[
            pl.BlockSpec((1, 1, rows, width), lambda i, j: (i, 0, j, 0)),
            pl.BlockSpec((parts, 1, tokens, width), lambda i, j: (0, 1, 0, 0)),
            pl.BlockSpec((parts, 1, tokens, width), lambda i, j: (0, 2, 0, 0)),
        ],
        out_specs=[
            pl.BlockSpec((1, rows, width), lambda i, j: (i, j, 0)),
            pl.BlockSpec((1, rows, width), lambda i, j: (i, j, 0)),
        ],
        out_shape=[
            jax.ShapeDtypeStruct((parts, tokens, width), BF16),
            jax.ShapeDtypeStruct((parts, tokens, width), F32),
        ],
        scratch_shapes=[pltpu.VMEM((parts * tokens, 2 * width), BF16)],
        cost_estimate=pl.CostEstimate(
            flops=2 * 512 * width // HD * (parts * tokens) ** 2,
            transcendentals=width // HD * (parts * tokens) ** 2,
            bytes_accessed=12 * parts * tokens * width,
        ),
        compiler_params=pltpu.CompilerParams(vmem_limit_bytes=VMEM_BYTES),
    )(packed, packed, packed)


def attend_back_kernel(q_ref, k_ref, v_ref, o_ref, g_ref, lse_ref, out_ref, dk_ref, dv_ref):
    part, block = pl.program_id(0), pl.program_id(1)
    parts, tokens = k_ref.shape[0], k_ref.shape[2]
    rows, width = q_ref.shape[2], q_ref.shape[3]
    seq = parts * tokens

    @pl.when((part == 0) & (block == 0))
    def _():
        dk_ref[...] = jnp.zeros_like(dk_ref)
        dv_ref[...] = jnp.zeros_like(dv_ref)

    queries = q_ref[0, 0] * SCALE
    grads = g_ref[0]
    keys = k_ref[:, 0].reshape(seq, width)
    values = v_ref[:, 0].reshape(seq, width)
    product = grads.astype(F32) * o_ref[0].astype(F32)
    logs = lse_ref[0]
    query_rows = queries.T
    grad_rows = grads.T
    lane = lane_head(width)
    dquery = jnp.zeros((rows, width), F32)
    for head in range(width // HD):
        own = lane == head
        span = slice(head * HD, (head + 1) * HD)
        scores = times_transposed(jnp.where(own, queries, 0).astype(BF16), keys)
        weight = jnp.exp(scores - logs[:, head * HD : head * HD + 1])
        inner = jnp.sum(jnp.where(own, product, 0.0), axis=1, keepdims=True)
        weight_grad = times_transposed(jnp.where(own, grads, 0).astype(BF16), values)
        score_grad = (weight * (weight_grad - inner)).astype(BF16)
        dv_ref[span, :] += matmul(grad_rows[span], weight.astype(BF16))
        dk_ref[span, :] += matmul(query_rows[span], score_grad)
        dquery = jnp.where(own, matmul(score_grad, keys), dquery)
    out_ref[part, 0, pl.ds(pl.multiple_of(block * rows, rows), rows), :] = (dquery * SCALE).astype(BF16)

    @pl.when((part == parts - 1) & (block == pl.num_programs(1) - 1))
    def _():
        out_ref[:, 1] = dk_ref[...].T.astype(BF16).reshape(parts, tokens, width)
        out_ref[:, 2] = dv_ref[...].T.astype(BF16).reshape(parts, tokens, width)


def attend_back(packed, mixed, grads, logs):
    parts, _, tokens, width = packed.shape
    rows = block_rows(tokens)
    own = pl.BlockSpec((1, rows, width), lambda i, j: (i, j, 0))
    return pl.pallas_call(
        attend_back_kernel,
        name="attend_back",
        grid=(parts, tokens // rows),
        in_specs=[
            pl.BlockSpec((1, 1, rows, width), lambda i, j: (i, 0, j, 0)),
            pl.BlockSpec((parts, 1, tokens, width), lambda i, j: (0, 1, 0, 0)),
            pl.BlockSpec((parts, 1, tokens, width), lambda i, j: (0, 2, 0, 0)),
            own,
            own,
            own,
        ],
        out_specs=pl.BlockSpec((parts, 3, tokens, width), lambda i, j: (0, 0, 0, 0)),
        out_shape=jax.ShapeDtypeStruct((parts, 3, tokens, width), BF16),
        scratch_shapes=[
            pltpu.VMEM((width, parts * tokens), F32),
            pltpu.VMEM((width, parts * tokens), F32),
        ],
        cost_estimate=pl.CostEstimate(
            flops=5 * 512 * width // HD * (parts * tokens) ** 2,
            transcendentals=width // HD * (parts * tokens) ** 2,
            bytes_accessed=20 * parts * tokens * width,
        ),
        compiler_params=pltpu.CompilerParams(vmem_limit_bytes=VMEM_BYTES),
    )(packed, packed, packed, mixed, grads, logs)


def xor_order(pieces, index):
    count = pieces.shape[0]
    bit = 1
    while bit < count:
        split = pieces.reshape((count // (2 * bit), 2, bit) + pieces.shape[1:])
        pieces = jnp.where((index & bit) != 0, split[:, ::-1], split).reshape(pieces.shape)
        bit *= 2
    return pieces


def exchange(pieces):
    count = pieces.shape[0]
    return jnp.stack(
        [pieces[0]]
        + [lax.ppermute(pieces[k], "z", [(i, i ^ k) for i in range(count)]) for k in range(1, count)]
    )


def swap(value):
    return lax.ppermute(value, "c", [(0, 1), (1, 0)])


def with_partner(rows):
    return jnp.concatenate([rows, swap(rows)], axis=0)


def sum_with_partner(partial_rows):
    half = partial_rows.shape[0] // 2
    return partial_rows[:half] + swap(partial_rows[half:])


def add_rounded(left, right):
    return (left.astype(F32) + right.astype(F32)).astype(left.dtype)


def join_columns_kernel(core_ref, *refs, moves):
    out_ref = refs[-1]
    core = core_ref[0]
    for layer in range(out_ref.shape[0]):
        own_ref, other_ref = refs[2 * layer], refs[2 * layer + 1]
        for half in range(2):
            mine = core == half
            for source, target, size in moves:
                span = slice(source, source + size)
                part = jnp.where(mine, own_ref[:, span], other_ref[:, span])
                out_ref[layer, :, target[half] : target[half] + size] = part.astype(F32)


def join_columns(pairs, core, moves):
    rows, columns = pairs[0][0].shape
    block = 64 if rows % 64 == 0 else rows
    spec = pl.BlockSpec((block, columns), lambda i, core: (i, 0))
    return pl.pallas_call(
        partial(join_columns_kernel, moves=moves),
        name="join_columns",
        grid_spec=pltpu.PrefetchScalarGridSpec(
            num_scalar_prefetch=1,
            grid=(rows // block,),
            in_specs=[spec] * (2 * len(pairs)),
            out_specs=pl.BlockSpec((len(pairs), block, 2 * columns), lambda i, core: (0, i, 0)),
        ),
        out_shape=jax.ShapeDtypeStruct((len(pairs), rows, 2 * columns), F32),
        compiler_params=pltpu.CompilerParams(vmem_limit_bytes=VMEM_BYTES),
    )(core, *[part for pair in pairs for part in pair])


def join_rows_kernel(core_ref, *refs):
    out_ref = refs[-1]
    mine = core_ref[0] == pl.program_id(0)
    for layer in range(out_ref.shape[0]):
        out_ref[layer] = jnp.where(mine, refs[2 * layer][...], refs[2 * layer + 1][...]).astype(F32)


def join_rows(pairs, core):
    rows, columns = pairs[0][0].shape
    block = 128 if rows % 128 == 0 else rows
    count = rows // block
    spec = pl.BlockSpec((block, columns), lambda h, i, core: (i, 0))
    return pl.pallas_call(
        join_rows_kernel,
        name="join_rows",
        grid_spec=pltpu.PrefetchScalarGridSpec(
            num_scalar_prefetch=1,
            grid=(2, count),
            in_specs=[spec] * (2 * len(pairs)),
            out_specs=pl.BlockSpec((len(pairs), block, columns), lambda h, i, core: (0, h * count + i, 0)),
        ),
        out_shape=jax.ShapeDtypeStruct((len(pairs), 2 * rows, columns), F32),
        compiler_params=pltpu.CompilerParams(vmem_limit_bytes=VMEM_BYTES),
    )(core, *[part for pair in pairs for part in pair])


class Pipeline:
    def __init__(self):
        self.running = []
        self.finished = {}
        self.fresh = {}

    def add(self, flow, finish):
        self.running.append([flow, finish, None, None])

    def advance(self, main):
        due = []
        for item in self.running:
            if item[2] is not None:
                item[3] -= 1
            if item[2] is None or item[3] <= 0:
                due.append(item)
        flights = [item[2] for item in due]
        main, flights, fresh = lax.optimization_barrier((main, flights, self.fresh))
        self.finished.update(fresh)
        self.fresh = {}
        steps = []
        for item, flight in zip(due, flights):
            try:
                steps.append((item,) + item[0].send(flight))
            except StopIteration as stop:
                item[1](stop.value)
                self.running.remove(item)
        sends = [step[1] for step in steps]
        main, sends = lax.optimization_barrier((main, sends))
        for (item, _, start, hold), values in zip(steps, sends):
            item[2], item[3] = start(values), hold
        return main

    def drain(self):
        while self.running:
            self.advance(())
        self.finished.update(self.fresh)


def bit_count(number):
    return number.bit_length() - 1


def swap_pairs(count, bit):
    return [(i, i ^ (1 << bit)) for i in range(count)]


def pick(values, place, axis):
    return lax.dynamic_index_in_dim(values, place, axis, keepdims=False)


def scatter_flow(gradient, index, count):
    bits = bit_count(count)
    half = gradient.shape[1] // 2
    lead = (2,) * bits + (gradient.shape[0] // count,)
    halves = [gradient[:, :half].reshape(lead + (half,)), gradient[:, half:].reshape(lead + (half,))]
    for step in range(bits):
        places = [(bits - 1 - step, 0), (step, bits - 1 - step)]
        mine = [(index >> bit) & 1 for bit, _ in places]
        sends = [pick(value, 1 - own, axis) for value, own, (_, axis) in zip(halves, mine, places)]
        kept = [pick(value, own, axis) for value, own, (_, axis) in zip(halves, mine, places)]

        def start(values, places=places):
            return [
                lax.ppermute(value, "shard", swap_pairs(count, bit)) for value, (bit, _) in zip(values, places)
            ]

        arrived = yield sends, start, 1
        halves = [add_rounded(own, other) for own, other in zip(kept, arrived)]
    return jnp.concatenate(halves, axis=1)


def offload_flow(gradient, hold):
    def start(values):
        return [lax.psum_scatter(values[0], "shard", scatter_dimension=0, tiled=True)]

    (piece,) = yield [gradient], start, hold
    return piece


def line_flow(piece, count):
    total, carry = piece.astype(F32), None
    for step in range(1, count):
        pairs = [(step - 1, step), (count - step, count - step - 1)]
        send = piece if carry is None else add_rounded(piece, carry)

        def start(values, pairs=pairs):
            return [lax.ppermute(values[0], "z", pairs)]

        (carry,) = yield [send], start, 1
        total = total + carry.astype(F32)
    return total.astype(piece.dtype)


def halving_flow(values, index, count):
    bits = bit_count(count)
    for bit in range(bits):
        upper = (index >> bit) & 1
        halves = values.reshape((2, values.shape[0] // 2) + values.shape[1:])

        def start(sent, bit=bit):
            return [lax.ppermute(sent[0], "z", swap_pairs(count, bit))]

        (other,) = yield [pick(halves, 1 - upper, 0)], start, 1
        values = add_rounded(pick(halves, upper, 0), other)
    for bit in reversed(range(bits)):
        upper = ((index >> bit) & 1) == 1

        def start(sent, bit=bit):
            return [lax.ppermute(sent[0], "z", swap_pairs(count, bit))]

        (other,) = yield [values], start, 1
        values = jnp.concatenate([jnp.where(upper, other, values), jnp.where(upper, values, other)], axis=0)
    return values


def gather_flow(part, index, count):
    bits = bit_count(count)
    half = part.shape[1] // 2
    halves = [part[:, :half], part[:, half:]]
    for step in range(bits):
        places = [(step, 0), (bits - 1 - step, step)]

        def start(values, places=places):
            return [
                lax.ppermute(value, "shard", swap_pairs(count, bit)) for value, (bit, _) in zip(values, places)
            ]

        arrived = yield halves, start, 1
        for place, (bit, axis) in enumerate(places):
            upper, own, other = ((index >> bit) & 1) == 1, halves[place], arrived[place]
            halves[place] = jnp.stack([jnp.where(upper, other, own), jnp.where(upper, own, other)], axis=axis)
    return jnp.concatenate([value.reshape(-1, half) for value in halves], axis=1)


def gelu_parts(pre_act):
    cdf = 0.5 * (1.0 + lax.erf(pre_act * (0.5**0.5)))
    density = jnp.exp(-0.5 * pre_act * pre_act) * 0.3989422804014327
    return (pre_act * cdf).astype(BF16), (cdf + pre_act * density).astype(BF16)


def body(
    images,
    norm1_scale,
    norm1_shift,
    qkv_weight,
    qv_bias,
    out_weight,
    out_bias,
    norm2_scale,
    norm2_shift,
    up_weight,
    up_bias,
    down_weight,
    down_bias,
    cotangent,
):
    image_count, local_len, width = images.shape
    z_count = lax.axis_size("z")
    shards = lax.axis_size("shard")
    z_index, c_index, s_index = lax.axis_index("z"), lax.axis_index("c"), lax.axis_index("shard")
    layers = norm1_scale.shape[0]
    hidden_units = up_bias.shape[1] * shards
    half_width = width // 2
    group = half_width // z_count
    tokens = 2 * local_len

    def my_half(values, axis):
        return lax.dynamic_index_in_dim(values, c_index, axis, keepdims=False)

    def gather(values):
        return lax.all_gather(values, "shard", axis=0, tiled=True)

    vectors = (norm1_scale, norm1_shift, out_bias, norm2_scale, norm2_shift, down_bias, qv_bias, up_bias)
    sizes = [member.shape[1] for member in vectors]
    offsets = [sum(sizes[:place]) for place in range(len(sizes) + 1)]
    vectors_full = lax.all_gather(jnp.concatenate(vectors, axis=1), "shard", axis=0)

    def full_vector(layer, place):
        return vectors_full[:, layer, offsets[place] : offsets[place + 1]].reshape(-1).astype(F32)

    pipeline = Pipeline()
    weights = []
    for layer in range(layers):
        qkv_part = my_half(qkv_weight[layer].reshape(-1, 3, shards, 2, half_width // shards), 3)
        qkv_part = jnp.swapaxes(qkv_part.reshape(-1, 3, z_count, group), 1, 2).reshape(-1, 3 * half_width)
        up_part = my_half(up_weight[layer].reshape(-1, shards, 2, hidden_units // 2 // shards), 2)
        held = {
            "out_part": my_half(out_weight[layer].reshape(2, -1, width), 0),
            "up": gather(up_part.reshape(-1, hidden_units // 2)),
            "down": gather(my_half(down_weight[layer].reshape(2, -1, width), 0)),
        }
        if layer == 0:
            held["qkv"] = gather(qkv_part)
        else:
            held["qkv_part"] = qkv_part
        weights.append(held)

    def fetch(layer, name):
        def finish(full):
            weights[layer][name] = full

        pipeline.add(gather_flow(weights[layer][name + "_part"], s_index, shards), finish)

    stream = images.astype(F32).reshape(-1, width)
    saved = []
    for layer in range(layers):
        held = weights[layer]
        scale_one, shift_one, out_shift, scale_two, shift_two, down_shift, qv_full, up_all = [
            full_vector(layer, place) for place in range(8)
        ]
        qv_halves = my_half(qv_full.reshape(2, shards, 2, half_width // shards), 2).reshape(2, z_count, group)
        qkv_shift = jnp.stack([qv_halves[0], jnp.zeros_like(qv_halves[0]), qv_halves[1]], axis=1).reshape(-1)
        up_shift = my_half(up_all.reshape(shards, 2, -1), 1).reshape(-1)

        if layer == 0:
            fetch(layer, "out")
        normed_own, average_one, inverse_one = norm_forward(stream, scale_one, shift_one)
        normed_own = pipeline.advance(normed_own)
        normed_one = with_partner(normed_own)
        projected = (matmul(normed_one, held["qkv"]) + qkv_shift).astype(BF16)
        pieces = projected.reshape(tokens, z_count, 3, group).transpose(1, 2, 0, 3)
        if layer + 1 < layers:
            fetch(layer + 1, "qkv")
        pieces = pipeline.advance(xor_order(pieces, z_index))
        packed = pipeline.advance(exchange(pieces))
        mixed, logs = attend(packed)
        while "out" not in held:
            mixed = pipeline.advance(mixed)
        attended = xor_order(exchange(mixed), z_index).transpose(1, 0, 2).reshape(tokens, half_width)
        middle = stream + sum_with_partner(matmul(attended, held["out"])) + out_shift
        if layer + 1 < layers:
            fetch(layer + 1, "out")
        middle = pipeline.advance(middle)
        two_own, average_two, inverse_two = norm_forward(middle, scale_two, shift_two)
        normed_two = with_partner(two_own)
        pre_act = matmul(normed_two, held["up"]) + up_shift
        hidden, slope = gelu_parts(pre_act)
        saved.append(
            (
                stream,
                average_one,
                inverse_one,
                normed_one,
                packed,
                mixed,
                logs,
                attended,
                middle,
                average_two,
                inverse_two,
                normed_two,
                hidden,
                slope,
                scale_one,
                scale_two,
            )
        )
        stream = middle + sum_with_partner(matmul(hidden, held["down"])) + down_shift
        stream = pipeline.advance(stream)
        while layer + 1 < layers and "qkv" not in weights[layer + 1]:
            stream = pipeline.advance(stream)
    results = stream.astype(BF16).reshape(image_count, local_len, width)

    core = c_index.astype(jnp.int32).reshape(1)
    block = half_width // shards
    cut = min(block, group)
    qkv_moves = []
    for part in range(3):
        for start in range(0, half_width, cut):
            source = start // group * 3 * group + part * group + start % group
            target = part * width + start // block * 2 * block + start % block
            qkv_moves.append((source, (target, target + block), cut))
    block_up = hidden_units // 2 // shards
    up_moves = [
        (place * block_up, (2 * place * block_up, (2 * place + 1) * block_up), block_up) for place in range(shards)
    ]

    joins = {
        "qkv": lambda pairs: join_columns(pairs, core, qkv_moves),
        "up": lambda pairs: join_columns(pairs, core, up_moves),
        "out": lambda pairs: join_rows(pairs, core),
        "down": lambda pairs: join_rows(pairs, core),
        "small": lambda pairs: jnp.stack([(own + other).reshape(-1) for own, other in pairs]),
    }
    weight_grads = [{} for _ in range(layers)]

    def reduce_flow(gradient, offloaded, hold, halving):
        if offloaded:
            piece = yield from offload_flow(gradient, hold)
        else:
            piece = yield from scatter_flow(gradient, s_index, shards)
        if halving:
            piece = yield from halving_flow(piece, z_index, z_count)
        else:
            piece = yield from line_flow(piece, z_count)
        (other,) = yield [piece], lambda values: [swap(values[0])], 1
        return piece, other

    def reduce_weight(layer, name, gradient, offloaded, hold=1, halving=False):
        def finish(pair):
            weight_grads[layer][name] = pair
            if all(name in done for done in weight_grads):
                pipeline.fresh[name] = joins[name]([done[name] for done in weight_grads])

        if name != "small":
            gradient = gradient.astype(BF16)
        pipeline.add(reduce_flow(gradient, offloaded, hold, halving), finish)

    grad_stream = cotangent.astype(F32).reshape(-1, width)
    for layer in reversed(range(layers)):
        (
            stream_in,
            average_one,
            inverse_one,
            normed_one,
            packed,
            mixed,
            logs,
            attended,
            middle,
            average_two,
            inverse_two,
            normed_two,
            hidden,
            slope,
            scale_one,
            scale_two,
        ) = saved[layer]
        held = weights[layer]
        offloaded = layer > 0
        branch_own = grad_stream.astype(BF16)
        branch_grad = with_partner(branch_own)
        grad_down_b = jnp.sum(branch_own.astype(F32), axis=0)
        reduce_weight(layer, "down", outer_sum(hidden, branch_grad), offloaded, 3, not offloaded)
        pre_grad = (times_transposed(branch_grad, held["down"]) * slope.astype(F32)).astype(BF16)
        pre_grad = pipeline.advance(pre_grad)
        two_grad = sum_with_partner(times_transposed(pre_grad, held["up"]))
        grad_up_b = jnp.sum(pre_grad.astype(F32), axis=0)
        middle_back, grad_scale_two, grad_shift_two = norm_backward(
            middle, average_two, inverse_two, scale_two, two_grad
        )
        middle_grad = grad_stream + middle_back
        out_own = middle_grad.astype(BF16)
        out_grad = with_partner(out_own)
        grad_out_b = jnp.sum(out_own.astype(F32), axis=0)
        attended_grad = times_transposed(out_grad, held["out"]).astype(BF16)
        grad_pieces = attended_grad.reshape(tokens, z_count, group).transpose(1, 0, 2)
        grad_pieces = pipeline.advance(xor_order(grad_pieces, z_index))
        head_grad = exchange(grad_pieces)
        reduce_weight(layer, "up", outer_sum(normed_two, pre_grad), offloaded, 3, not offloaded)
        head_grad = pipeline.advance(head_grad)
        heads_back = pipeline.advance(attend_back(packed, mixed, head_grad, logs))
        reduce_weight(layer, "out", outer_sum(attended, out_grad), offloaded, 3, not offloaded)
        arrived = pipeline.advance(exchange(heads_back))
        projected_grad = xor_order(arrived, z_index).transpose(2, 0, 1, 3)
        projected_grad = projected_grad.reshape(tokens, 3 * half_width)
        one_grad = sum_with_partner(times_transposed(projected_grad, held["qkv"]))
        reduce_weight(layer, "qkv", outer_sum(normed_one, projected_grad), offloaded, 4, not offloaded)
        column_sums = jnp.sum(projected_grad.astype(F32), axis=0).reshape(z_count, 3, group)
        grad_qv_b = jnp.stack([column_sums[:, 0], column_sums[:, 2]])
        stream_back, grad_scale_one, grad_shift_one = norm_backward(
            stream_in, average_one, inverse_one, scale_one, one_grad
        )
        grad_stream = middle_grad + stream_back

        def spread(values, lead):
            values = values.reshape(lead, shards, 1, -1)
            nothing = jnp.zeros_like(values)
            halves = jnp.concatenate(
                [
                    jnp.where(c_index == 0, values, nothing),
                    jnp.where(c_index == 0, nothing, values),
                ],
                axis=2,
            )
            return halves.reshape(shards, -1)

        small = jnp.concatenate(
            [
                member.reshape(shards, -1)
                for member in (
                    grad_scale_one,
                    grad_shift_one,
                    grad_out_b,
                    grad_scale_two,
                    grad_shift_two,
                    grad_down_b,
                    spread(grad_qv_b, 2),
                    spread(grad_up_b, 1),
                )
            ],
            axis=1,
        )
        reduce_weight(layer, "small", small.reshape(4 * shards, -1), False)
        grad_stream = pipeline.advance(grad_stream)

    pipeline.drain()
    sums = pipeline.finished
    vector_grads = [sums["small"][:, offsets[place] : offsets[place + 1]] for place in range(8)]
    grad_qkv, grad_out, grad_up, grad_down = sums["qkv"], sums["out"], sums["up"], sums["down"]
    input_grad = grad_stream.reshape(image_count, local_len, width)
    return (
        results,
        input_grad,
        vector_grads[0],
        vector_grads[1],
        grad_qkv,
        vector_grads[6],
        grad_out,
        vector_grads[2],
        vector_grads[3],
        vector_grads[4],
        grad_up,
        vector_grads[7],
        grad_down,
        vector_grads[5],
    )


def solution(mesh):
    seq, shards = mesh.devices.shape
    cores = Mesh(mesh.devices.reshape(seq // 2, 2, shards), ("z", "c", "shard"))
    rows = P("shard", ("z", "c"), None)
    vector = P(None, "shard")
    matrix = P(None, "shard", None)
    parameters = (
        vector,
        vector,
        matrix,
        vector,
        matrix,
        vector,
        vector,
        vector,
        matrix,
        vector,
        matrix,
        vector,
    )
    return jax.shard_map(
        body,
        mesh=cores,
        in_specs=(rows,) + parameters + (rows,),
        out_specs=(rows, rows) + parameters,
        check_vma=False,
    )
```

```python
from functools import partial

import jax
import jax.numpy as jnp
from jax import lax
from jax.experimental import pallas as pl
from jax.experimental.pallas import tpu as pltpu
from jax.sharding import Mesh
from jax.sharding import PartitionSpec as P

HD = 64
SCALE = HD ** (-0.5)
F32 = jnp.float32
BF16 = jnp.bfloat16
LANES = 512
VMEM_BYTES = 56 * 1024 * 1024


def matmul(left, right):
    return jnp.dot(left, right, preferred_element_type=F32)


def outer_sum(left, right):
    return lax.dot_general(left, right, (((0,), (0,)), ((), ())), preferred_element_type=F32)


def times_transposed(left, right):
    return lax.dot_general(left, right, (((1,), (1,)), ((), ())), preferred_element_type=F32)


def norm_forward(stream, scales, offset):
    average = jnp.mean(stream, axis=-1, keepdims=True)
    centered = stream - average
    variance = jnp.mean(centered * centered, axis=-1, keepdims=True)
    inverse = lax.rsqrt(variance + 1e-06)
    return (centered * inverse * scales + offset).astype(BF16), average, inverse


def norm_backward(stream, average, inverse, scales, upstream):
    unit_rows = (stream - average) * inverse
    grad_scale = jnp.sum(upstream * unit_rows, axis=0)
    grad_shift = jnp.sum(upstream, axis=0)
    scaled_grad = upstream * scales
    stream_grad = inverse * (
        scaled_grad
        - jnp.mean(scaled_grad, axis=-1, keepdims=True)
        - unit_rows * jnp.mean(scaled_grad * unit_rows, axis=-1, keepdims=True)
    )
    return stream_grad, grad_scale, grad_shift


def block_rows(tokens):
    for rows in (288, 192, 144, 96, 48, 16):
        if tokens % rows == 0:
            return rows
    return tokens


def lane_head(width):
    return lax.broadcasted_iota(jnp.int32, (1, width), 1) // HD


def attend_kernel(q_ref, k_ref, v_ref, o_ref, lse_ref, ext_ref):
    width = q_ref.shape[-1]
    seq = ext_ref.shape[0]

    @pl.when((pl.program_id(0) == 0) & (pl.program_id(1) == 0))
    def _():
        ext_ref[:, :width] = v_ref[:, 0].reshape(seq, width)
        ext_ref[:, width:] = jnp.ones((seq, ext_ref.shape[1] - width), BF16)

    queries = q_ref[0, 0] * SCALE
    keys = k_ref[:, 0].reshape(seq, width)
    lane = lane_head(width)
    mixed = jnp.zeros(queries.shape, F32)
    logs = jnp.zeros(queries.shape, F32)
    for head in range(width // HD):
        own = lane == head
        scores = times_transposed(jnp.where(own, queries, 0).astype(BF16), keys)
        row_max = jnp.max(scores, axis=1, keepdims=True)
        weight = jnp.exp(scores - row_max).astype(BF16)
        total = matmul(weight, ext_ref[...])
        row_total = total[:, width : 2 * width]
        mixed = jnp.where(own, total[:, :width] / row_total, mixed)
        logs = jnp.where(own, row_max + jnp.log(row_total), logs)
    o_ref[0] = mixed.astype(BF16)
    lse_ref[0] = logs


def attend(packed):
    parts, _, tokens, width = packed.shape
    rows = block_rows(tokens)
    return pl.pallas_call(
        attend_kernel,
        name="attend",
        grid=(parts, tokens // rows),
        in_specs=[
            pl.BlockSpec((1, 1, rows, width), lambda i, j: (i, 0, j, 0)),
            pl.BlockSpec((parts, 1, tokens, width), lambda i, j: (0, 1, 0, 0)),
            pl.BlockSpec((parts, 1, tokens, width), lambda i, j: (0, 2, 0, 0)),
        ],
        out_specs=[
            pl.BlockSpec((1, rows, width), lambda i, j: (i, j, 0)),
            pl.BlockSpec((1, rows, width), lambda i, j: (i, j, 0)),
        ],
        out_shape=[
            jax.ShapeDtypeStruct((parts, tokens, width), BF16),
            jax.ShapeDtypeStruct((parts, tokens, width), F32),
        ],
        scratch_shapes=[pltpu.VMEM((parts * tokens, 2 * width), BF16)],
        cost_estimate=pl.CostEstimate(
            flops=2 * 512 * width // HD * (parts * tokens) ** 2,
            transcendentals=width // HD * (parts * tokens) ** 2,
            bytes_accessed=12 * parts * tokens * width,
        ),
        compiler_params=pltpu.CompilerParams(vmem_limit_bytes=VMEM_BYTES),
    )(packed, packed, packed)


def attend_back_kernel(q_ref, k_ref, v_ref, o_ref, g_ref, lse_ref, out_ref, dk_ref, dv_ref):
    part, block = pl.program_id(0), pl.program_id(1)
    parts, tokens = k_ref.shape[0], k_ref.shape[2]
    rows, width = q_ref.shape[2], q_ref.shape[3]
    seq = parts * tokens

    @pl.when((part == 0) & (block == 0))
    def _():
        dk_ref[...] = jnp.zeros_like(dk_ref)
        dv_ref[...] = jnp.zeros_like(dv_ref)

    queries = q_ref[0, 0] * SCALE
    grads = g_ref[0]
    keys = k_ref[:, 0].reshape(seq, width)
    values = v_ref[:, 0].reshape(seq, width)
    product = grads.astype(F32) * o_ref[0].astype(F32)
    logs = lse_ref[0]
    query_rows = queries.T
    grad_rows = grads.T
    lane = lane_head(width)
    dquery = jnp.zeros((rows, width), F32)
    for head in range(width // HD):
        own = lane == head
        span = slice(head * HD, (head + 1) * HD)
        scores = times_transposed(jnp.where(own, queries, 0).astype(BF16), keys)
        weight = jnp.exp(scores - logs[:, head * HD : head * HD + 1])
        inner = jnp.sum(jnp.where(own, product, 0.0), axis=1, keepdims=True)
        weight_grad = times_transposed(jnp.where(own, grads, 0).astype(BF16), values)
        score_grad = (weight * (weight_grad - inner)).astype(BF16)
        dv_ref[span, :] += matmul(grad_rows[span], weight.astype(BF16))
        dk_ref[span, :] += matmul(query_rows[span], score_grad)
        dquery = jnp.where(own, matmul(score_grad, keys), dquery)
    out_ref[part, 0, pl.ds(pl.multiple_of(block * rows, rows), rows), :] = (dquery * SCALE).astype(BF16)

    @pl.when((part == parts - 1) & (block == pl.num_programs(1) - 1))
    def _():
        out_ref[:, 1] = dk_ref[...].T.astype(BF16).reshape(parts, tokens, width)
        out_ref[:, 2] = dv_ref[...].T.astype(BF16).reshape(parts, tokens, width)


def attend_back(packed, mixed, grads, logs):
    parts, _, tokens, width = packed.shape
    rows = block_rows(tokens)
    own = pl.BlockSpec((1, rows, width), lambda i, j: (i, j, 0))
    return pl.pallas_call(
        attend_back_kernel,
        name="attend_back",
        grid=(parts, tokens // rows),
        in_specs=[
            pl.BlockSpec((1, 1, rows, width), lambda i, j: (i, 0, j, 0)),
            pl.BlockSpec((parts, 1, tokens, width), lambda i, j: (0, 1, 0, 0)),
            pl.BlockSpec((parts, 1, tokens, width), lambda i, j: (0, 2, 0, 0)),
            own,
            own,
            own,
        ],
        out_specs=pl.BlockSpec((parts, 3, tokens, width), lambda i, j: (0, 0, 0, 0)),
        out_shape=jax.ShapeDtypeStruct((parts, 3, tokens, width), BF16),
        scratch_shapes=[
            pltpu.VMEM((width, parts * tokens), F32),
            pltpu.VMEM((width, parts * tokens), F32),
        ],
        cost_estimate=pl.CostEstimate(
            flops=5 * 512 * width // HD * (parts * tokens) ** 2,
            transcendentals=width // HD * (parts * tokens) ** 2,
            bytes_accessed=20 * parts * tokens * width,
        ),
        compiler_params=pltpu.CompilerParams(vmem_limit_bytes=VMEM_BYTES),
    )(packed, packed, packed, mixed, grads, logs)


def xor_order(pieces, index):
    count = pieces.shape[0]
    bit = 1
    while bit < count:
        split = pieces.reshape((count // (2 * bit), 2, bit) + pieces.shape[1:])
        pieces = jnp.where((index & bit) != 0, split[:, ::-1], split).reshape(pieces.shape)
        bit *= 2
    return pieces


def exchange(pieces):
    count = pieces.shape[0]
    return jnp.stack(
        [pieces[0]]
        + [lax.ppermute(pieces[k], "z", [(i, i ^ k) for i in range(count)]) for k in range(1, count)]
    )


def swap(value):
    return lax.ppermute(value, "c", [(0, 1), (1, 0)])


def with_partner(rows):
    return jnp.concatenate([rows, swap(rows)], axis=0)


def sum_with_partner(partial_rows):
    half = partial_rows.shape[0] // 2
    return partial_rows[:half] + swap(partial_rows[half:])


def add_rounded(left, right):
    return (left.astype(F32) + right.astype(F32)).astype(left.dtype)


def merge(pieces):
    blocks = [piece[:, start : start + LANES] for piece in pieces for start in range(0, piece.shape[1], LANES)]
    return jnp.concatenate([block.astype(BF16) for block in blocks], axis=0)


def join_kernel(core_ref, *refs, moves, count):
    out_ref = refs[-1]
    for layer in range(out_ref.shape[0]):
        blocks = refs[2 * count * layer : 2 * count * (layer + 1)]
        for half, source, target, size in moves:
            mine = core_ref[0] == (pl.program_id(0) if half is None else half)
            place, start = source // LANES, source % LANES
            span = slice(start, start + size)
            part = jnp.where(mine, blocks[place][:, span], blocks[count + place][:, span])
            out_ref[layer, :, target : target + size] = part.astype(F32)


def join(pairs, core, rows, columns, offsets, moves, by_rows):
    count = columns // LANES
    block = next(size for size in (64, 32, 16, 8) if rows % size == 0)
    steps = rows // block
    specs, operands = [], []
    for pair, offset in zip(pairs, offsets):
        for member in pair:
            for place in range(count):
                first = offset // block + place * steps
                specs.append(pl.BlockSpec((block, LANES), lambda h, i, core, first=first: (first + i, 0)))
                operands.append(member)
    if by_rows:
        grid, shape = (2, steps), (len(pairs), 2 * rows, columns)
    else:
        grid, shape = (1, steps), (len(pairs), rows, 2 * columns)
    return pl.pallas_call(
        partial(join_kernel, moves=moves, count=count),
        name="join",
        grid_spec=pltpu.PrefetchScalarGridSpec(
            num_scalar_prefetch=1,
            grid=grid,
            in_specs=specs,
            out_specs=pl.BlockSpec((len(pairs), block, shape[2]), lambda h, i, core: (0, h * steps + i, 0)),
        ),
        out_shape=jax.ShapeDtypeStruct(shape, F32),
        compiler_params=pltpu.CompilerParams(vmem_limit_bytes=VMEM_BYTES),
    )(core, *operands)


class Pipeline:
    def __init__(self):
        self.running = []
        self.finished = {}
        self.fresh = {}

    def add(self, flow, finish):
        self.running.append([flow, finish, None, ""])

    def advance(self, main, point=None, last=False):
        due = []
        for item in self.running:
            if isinstance(item[3], int):
                item[3] -= 1
            if item[2] is None or last or item[3] == 0 or item[3] == point:
                due.append(item)
        flights = [item[2] for item in due]
        main, flights, fresh = lax.optimization_barrier((main, flights, self.fresh))
        self.finished.update(fresh)
        self.fresh = {}
        steps = []
        waiting = list(zip(due, flights))
        while waiting:
            item, flight = waiting.pop(0)
            try:
                steps.append((item,) + item[0].send(flight))
            except StopIteration as stop:
                self.running.remove(item)
                known = len(self.running)
                item[1](stop.value)
                waiting += [(added, None) for added in self.running[known:]]
        sends = [step[1] for step in steps]
        main, sends = lax.optimization_barrier((main, sends))
        for (item, _, start, hold), values in zip(steps, sends):
            item[2], item[3] = start(values), hold
        return main

    def drain(self):
        while self.running:
            self.advance((), last=True)
        self.finished.update(self.fresh)


def bit_count(number):
    return number.bit_length() - 1


def swap_pairs(count, bit):
    return [(i, i ^ (1 << bit)) for i in range(count)]


def pick(values, place, axis):
    return lax.dynamic_index_in_dim(values, place, axis, keepdims=False)


def pause(point):
    yield [], lambda values: [], point


def scatter_flow(gradient, index, count, points):
    bits = bit_count(count)
    half = gradient.shape[1] // 2
    lead = (2,) * bits + (gradient.shape[0] // count,)
    halves = [gradient[:, :half].reshape(lead + (half,)), gradient[:, half:].reshape(lead + (half,))]
    for step in range(bits):
        places = [(bits - 1 - step, 0), (step, bits - 1 - step)]
        mine = [(index >> bit) & 1 for bit, _ in places]
        sends = [pick(value, 1 - own, axis) for value, own, (_, axis) in zip(halves, mine, places)]
        kept = [pick(value, own, axis) for value, own, (_, axis) in zip(halves, mine, places)]

        def start(values, places=places):
            return [
                lax.ppermute(value, "shard", swap_pairs(count, bit)) for value, (bit, _) in zip(values, places)
            ]

        arrived = yield sends, start, points[min(step, len(points) - 1)]
        halves = [add_rounded(own, other) for own, other in zip(kept, arrived)]
    return jnp.concatenate(halves, axis=1)


def offload_flow(gradient, point):
    def start(values):
        return [lax.psum_scatter(values[0], "shard", scatter_dimension=0, tiled=True)]

    (piece,) = yield [gradient], start, point
    return piece


def line_flow(piece, count, points):
    total, carry = piece.astype(F32), None
    for step in range(1, count):
        begin, point = points[step - 1] if step <= len(points) else ("", 1)
        if begin:
            yield from pause(begin)
        pairs = [(step - 1, step), (count - step, count - step - 1)]
        send = piece if carry is None else add_rounded(piece, carry)

        def start(values, pairs=pairs):
            return [lax.ppermute(values[0], "z", pairs)]

        (carry,) = yield [send], start, point
        total = total + carry.astype(F32)
    return total.astype(piece.dtype)


def gather_flow(part, index, count, holds):
    bits = bit_count(count)
    half = part.shape[1] // 2
    halves = [part[:, :half], part[:, half:]]
    for step in range(bits):
        places = [(step, 0), (bits - 1 - step, step)]

        def start(values, places=places):
            return [
                lax.ppermute(value, "shard", swap_pairs(count, bit)) for value, (bit, _) in zip(values, places)
            ]

        arrived = yield halves, start, holds[min(step, len(holds) - 1)]
        for place, (bit, axis) in enumerate(places):
            upper, own, other = ((index >> bit) & 1) == 1, halves[place], arrived[place]
            halves[place] = jnp.stack([jnp.where(upper, other, own), jnp.where(upper, own, other)], axis=axis)
    return jnp.concatenate([value.reshape(-1, half) for value in halves], axis=1)


def gelu_parts(pre_act):
    cdf = 0.5 * (1.0 + lax.erf(pre_act * (0.5**0.5)))
    density = jnp.exp(-0.5 * pre_act * pre_act) * 0.3989422804014327
    return (pre_act * cdf).astype(BF16), (cdf + pre_act * density).astype(BF16)


def body(
    images,
    norm1_scale,
    norm1_shift,
    qkv_weight,
    qv_bias,
    out_weight,
    out_bias,
    norm2_scale,
    norm2_shift,
    up_weight,
    up_bias,
    down_weight,
    down_bias,
    cotangent,
):
    image_count, local_len, width = images.shape
    z_count = lax.axis_size("z")
    shards = lax.axis_size("shard")
    z_index, c_index, s_index = lax.axis_index("z"), lax.axis_index("c"), lax.axis_index("shard")
    layers = norm1_scale.shape[0]
    hidden_units = up_bias.shape[1] * shards
    half_width = width // 2
    group = half_width // z_count
    tokens = 2 * local_len

    def my_half(values, axis):
        return lax.dynamic_index_in_dim(values, c_index, axis, keepdims=False)

    def gather(values):
        return lax.all_gather(values, "shard", axis=0, tiled=True)

    vectors = (norm1_scale, norm1_shift, out_bias, norm2_scale, norm2_shift, down_bias, qv_bias, up_bias)
    sizes = [member.shape[1] for member in vectors]
    offsets = [sum(sizes[:place]) for place in range(len(sizes) + 1)]
    vectors_full = lax.all_gather(jnp.concatenate(vectors, axis=1), "shard", axis=0)

    def full_vector(layer, place):
        return vectors_full[:, layer, offsets[place] : offsets[place + 1]].reshape(-1).astype(F32)

    pipeline = Pipeline()
    weights = []
    for layer in range(layers):
        qkv_part = my_half(qkv_weight[layer].reshape(-1, 3, shards, 2, half_width // shards), 3)
        qkv_part = jnp.swapaxes(qkv_part.reshape(-1, 3, z_count, group), 1, 2).reshape(-1, 3 * half_width)
        up_part = my_half(up_weight[layer].reshape(-1, shards, 2, hidden_units // 2 // shards), 2)
        held = {
            "out_part": my_half(out_weight[layer].reshape(2, -1, width), 0),
            "up": gather(up_part.reshape(-1, hidden_units // 2)),
            "down": gather(my_half(down_weight[layer].reshape(2, -1, width), 0)),
        }
        if layer == 0:
            held["qkv"] = gather(qkv_part)
        else:
            held["qkv_part"] = qkv_part
        weights.append(held)

    def fetch(layer, name, holds=(1,)):
        def finish(full):
            weights[layer][name] = full

        pipeline.add(gather_flow(weights[layer][name + "_part"], s_index, shards, holds), finish)

    stream = images.astype(F32).reshape(-1, width)
    saved = []
    for layer in range(layers):
        held = weights[layer]
        scale_one, shift_one, out_shift, scale_two, shift_two, down_shift, qv_full, up_all = [
            full_vector(layer, place) for place in range(8)
        ]
        qv_halves = my_half(qv_full.reshape(2, shards, 2, half_width // shards), 2).reshape(2, z_count, group)
        qkv_shift = jnp.stack([qv_halves[0], jnp.zeros_like(qv_halves[0]), qv_halves[1]], axis=1).reshape(-1)
        up_shift = my_half(up_all.reshape(shards, 2, -1), 1).reshape(-1)

        if layer == 0:
            fetch(layer, "out")
        normed_own, average_one, inverse_one = norm_forward(stream, scale_one, shift_one)
        normed_own = pipeline.advance(normed_own)
        normed_one = with_partner(normed_own)
        projected = (matmul(normed_one, held["qkv"]) + qkv_shift).astype(BF16)
        pieces = projected.reshape(tokens, z_count, 3, group).transpose(1, 2, 0, 3)
        if layer + 1 < layers:
            fetch(layer + 1, "qkv")
        pieces = pipeline.advance(xor_order(pieces, z_index))
        packed = pipeline.advance(exchange(pieces))
        mixed, logs = attend(packed)
        mixed = pipeline.advance(mixed)
        while "out" not in held:
            mixed = pipeline.advance(mixed)
        attended = xor_order(exchange(mixed), z_index).transpose(1, 0, 2).reshape(tokens, half_width)
        middle = stream + sum_with_partner(matmul(attended, held["out"])) + out_shift
        if layer + 1 < layers:
            fetch(layer + 1, "out", (1, 3))
        middle = pipeline.advance(middle)
        two_own, average_two, inverse_two = norm_forward(middle, scale_two, shift_two)
        normed_two = with_partner(two_own)
        pre_act = matmul(normed_two, held["up"]) + up_shift
        hidden, slope = gelu_parts(pre_act)
        saved.append(
            (
                stream,
                average_one,
                inverse_one,
                normed_one,
                packed,
                mixed,
                logs,
                attended,
                middle,
                average_two,
                inverse_two,
                normed_two,
                hidden,
                slope,
                scale_one,
                scale_two,
            )
        )
        stream = middle + sum_with_partner(matmul(hidden, held["down"])) + down_shift
        stream = pipeline.advance(stream)
        while layer + 1 < layers and "qkv" not in weights[layer + 1]:
            stream = pipeline.advance(stream)
    results = stream.astype(BF16).reshape(image_count, local_len, width)

    core = c_index.astype(jnp.int32).reshape(1)
    block = half_width // shards
    cut = min(block, group)
    qkv_moves = []
    for part in range(3):
        for start in range(0, half_width, cut):
            source = start // group * 3 * group + part * group + start % group
            target = part * width + start // block * 2 * block + start % block
            qkv_moves += [(core_of, source, target + core_of * block, cut) for core_of in range(2)]
    block_up = hidden_units // 2 // shards
    up_moves = [
        (core_of, place * block_up, (2 * place + core_of) * block_up, block_up)
        for place in range(shards)
        for core_of in range(2)
    ]
    row_moves = [(None, start, start, LANES) for start in range(0, width, LANES)]
    local = width // shards
    forms = {
        "down": (hidden_units // 2 // shards, width, row_moves, True),
        "up": (local, hidden_units // 2, up_moves, False),
        "out": (half_width // shards, width, row_moves, True),
        "qkv": (local, 3 * half_width, qkv_moves, False),
    }
    small_rows = 64
    groups = [
        [("down",), ("up",)] + ([("out", "qkv"), ("small",)] if layer == 0 else [("out", "qkv", "small")])
        for layer in range(layers)
    ]

    def line_points(layer, name):
        if layer == 0:
            return [("", "end0")] if name == "down" else []
        end, later = f"end{layer}", f"end{layer - 1}"
        b, c, d, e = [f"{kind}{layer - 1}" for kind in "bcde"]
        return {
            "down": [("", end), ("", b), (c, d)],
            "up": [("", b), (c, d), (e, later)],
            "out": [("", d), (e, later)],
        }[name]

    pieces_of = [{} for _ in range(layers)]
    sums_of = [{} for _ in range(layers)]

    def total_flow(merged, points):
        merged = yield from line_flow(merged, z_count, points)
        (other,) = yield [merged], lambda values: [swap(values[0])], 1
        return merged, other

    def arrived_in(layer, name, piece):
        pieces_of[layer][name] = piece
        for names in groups[layer]:
            if name in names and all(member in pieces_of[layer] for member in names):
                members = [pieces_of[layer][member] for member in names]
                flow = total_flow(merge(members), line_points(layer, names[0]))
                pipeline.add(flow, partial(summed, layer, names, [member.size // LANES for member in members]))

    def summed(layer, names, extents, pair):
        offset = 0
        for name, extent in zip(names, extents):
            sums_of[layer][name] = (pair, offset)
            offset += extent
            if all(name in sums for sums in sums_of):
                pairs = [sums[name][0] for sums in sums_of]
                starts = [sums[name][1] for sums in sums_of]
                if name == "small":
                    count = offsets[-1] // LANES
                    pipeline.fresh[name] = jnp.stack(
                        [
                            sum(member[start : start + count].astype(F32) for member in pair).reshape(-1)
                            for pair, start in zip(pairs, starts)
                        ]
                    )
                else:
                    rows, columns, moves, by_rows = forms[name]
                    pipeline.fresh[name] = join(pairs, core, rows, columns, starts, moves, by_rows)

    def reduce_weight(layer, name, gradient, points):
        if name != "small":
            gradient = gradient.astype(BF16)
        if isinstance(points, tuple):
            flow = scatter_flow(gradient, s_index, shards, points)
        else:
            flow = offload_flow(gradient, points)
        pipeline.add(flow, partial(arrived_in, layer, name))

    grad_stream = cotangent.astype(F32).reshape(-1, width)
    for layer in reversed(range(layers)):
        (
            stream_in,
            average_one,
            inverse_one,
            normed_one,
            packed,
            mixed,
            logs,
            attended,
            middle,
            average_two,
            inverse_two,
            normed_two,
            hidden,
            slope,
            scale_one,
            scale_two,
        ) = saved[layer]
        held = weights[layer]
        late = layer == 0
        branch_own = grad_stream.astype(BF16)
        branch_grad = with_partner(branch_own)
        grad_down_b = jnp.sum(branch_own.astype(F32), axis=0)
        if not late:
            reduce_weight(layer, "down", outer_sum(hidden, branch_grad), f"e{layer}")
        pre_grad = (times_transposed(branch_grad, held["down"]) * slope.astype(F32)).astype(BF16)
        two_grad = sum_with_partner(times_transposed(pre_grad, held["up"]))
        grad_up_b = jnp.sum(pre_grad.astype(F32), axis=0)
        middle_back, grad_scale_two, grad_shift_two = norm_backward(
            middle, average_two, inverse_two, scale_two, two_grad
        )
        middle_grad = grad_stream + middle_back
        out_own = middle_grad.astype(BF16)
        out_grad = with_partner(out_own)
        grad_out_b = jnp.sum(out_own.astype(F32), axis=0)
        attended_grad = times_transposed(out_grad, held["out"]).astype(BF16)
        grad_pieces = attended_grad.reshape(tokens, z_count, group).transpose(1, 0, 2)
        grad_pieces = pipeline.advance(xor_order(grad_pieces, z_index), f"b{layer}")
        head_grad = exchange(grad_pieces)
        reduce_weight(layer, "up", outer_sum(normed_two, pre_grad), f"end{layer}")
        if late:
            reduce_weight(layer, "down", outer_sum(hidden, branch_grad), (f"d{layer}", f"e{layer}"))
            reduce_weight(layer, "out", outer_sum(attended, out_grad), f"end{layer}")
        head_grad = pipeline.advance(head_grad, f"c{layer}")
        heads_back = pipeline.advance(attend_back(packed, mixed, head_grad, logs), f"d{layer}")
        if not late:
            reduce_weight(layer, "out", outer_sum(attended, out_grad), f"c{layer - 1}")
        arrived = pipeline.advance(exchange(heads_back), f"e{layer}")
        projected_grad = xor_order(arrived, z_index).transpose(2, 0, 1, 3)
        projected_grad = projected_grad.reshape(tokens, 3 * half_width)
        qkv_points = (f"end{layer}", 1) if late else f"c{layer - 1}"
        reduce_weight(layer, "qkv", outer_sum(normed_one, projected_grad), qkv_points)
        if late:
            projected_grad = pipeline.advance(projected_grad, f"q{layer}")
        one_grad = sum_with_partner(times_transposed(projected_grad, held["qkv"]))
        column_sums = jnp.sum(projected_grad.astype(F32), axis=0).reshape(z_count, 3, group)
        grad_qv_b = jnp.stack([column_sums[:, 0], column_sums[:, 2]])
        stream_back, grad_scale_one, grad_shift_one = norm_backward(
            stream_in, average_one, inverse_one, scale_one, one_grad
        )
        grad_stream = middle_grad + stream_back

        def spread(values, lead):
            values = values.reshape(lead, shards, 1, -1)
            nothing = jnp.zeros_like(values)
            halves = jnp.concatenate(
                [
                    jnp.where(c_index == 0, values, nothing),
                    jnp.where(c_index == 0, nothing, values),
                ],
                axis=2,
            )
            return halves.reshape(shards, -1)

        small = jnp.concatenate(
            [
                member.reshape(shards, -1)
                for member in (
                    grad_scale_one,
                    grad_shift_one,
                    grad_out_b,
                    grad_scale_two,
                    grad_shift_two,
                    grad_down_b,
                    spread(grad_qv_b, 2),
                    spread(grad_up_b, 1),
                )
            ],
            axis=1,
        )
        small = jnp.pad(small.reshape(shards, -1, LANES), ((0, 0), (0, small_rows - offsets[-1] // LANES), (0, 0)))
        reduce_weight(layer, "small", small.reshape(-1, LANES), 1 if late else f"c{layer - 1}")
        grad_stream = pipeline.advance(grad_stream, f"end{layer}")

    pipeline.drain()
    sums = pipeline.finished
    vector_grads = [sums["small"][:, offsets[place] : offsets[place + 1]] for place in range(8)]
    grad_qkv, grad_out, grad_up, grad_down = sums["qkv"], sums["out"], sums["up"], sums["down"]
    input_grad = grad_stream.reshape(image_count, local_len, width)
    return (
        results,
        input_grad,
        vector_grads[0],
        vector_grads[1],
        grad_qkv,
        vector_grads[6],
        grad_out,
        vector_grads[2],
        vector_grads[3],
        vector_grads[4],
        grad_up,
        vector_grads[7],
        grad_down,
        vector_grads[5],
    )


def solution(mesh):
    seq, shards = mesh.devices.shape
    cores = Mesh(mesh.devices.reshape(seq // 2, 2, shards), ("z", "c", "shard"))
    rows = P("shard", ("z", "c"), None)
    vector = P(None, "shard")
    matrix = P(None, "shard", None)
    parameters = (
        vector,
        vector,
        matrix,
        vector,
        matrix,
        vector,
        vector,
        vector,
        matrix,
        vector,
        matrix,
        vector,
    )
    return jax.shard_map(
        body,
        mesh=cores,
        in_specs=(rows,) + parameters + (rows,),
        out_specs=(rows, rows) + parameters,
        check_vma=False,
    )
```

```python
from functools import partial

import jax
import jax.numpy as jnp
from jax import lax
from jax.experimental import pallas as pl
from jax.experimental.pallas import tpu as pltpu
from jax.sharding import Mesh
from jax.sharding import PartitionSpec as P

HD = 64
SCALE = HD ** (-0.5)
F32 = jnp.float32
BF16 = jnp.bfloat16
LANES = 512
VMEM_BYTES = 56 * 1024 * 1024


def matmul(left, right):
    return jnp.dot(left, right, preferred_element_type=F32)


def outer_sum(left, right):
    return lax.dot_general(left, right, (((0,), (0,)), ((), ())), preferred_element_type=F32)


def times_transposed(left, right):
    return lax.dot_general(left, right, (((1,), (1,)), ((), ())), preferred_element_type=F32)


def norm_forward(stream, scales, offset):
    average = jnp.mean(stream, axis=-1, keepdims=True)
    centered = stream - average
    variance = jnp.mean(centered * centered, axis=-1, keepdims=True)
    inverse = lax.rsqrt(variance + 1e-06)
    return (centered * inverse * scales + offset).astype(BF16), average, inverse


def norm_backward(stream, average, inverse, scales, upstream):
    unit_rows = (stream - average) * inverse
    grad_scale = jnp.sum(upstream * unit_rows, axis=0)
    grad_shift = jnp.sum(upstream, axis=0)
    scaled_grad = upstream * scales
    stream_grad = inverse * (
        scaled_grad
        - jnp.mean(scaled_grad, axis=-1, keepdims=True)
        - unit_rows * jnp.mean(scaled_grad * unit_rows, axis=-1, keepdims=True)
    )
    return stream_grad, grad_scale, grad_shift


def block_rows(tokens):
    for rows in (288, 192, 144, 96, 48, 16):
        if tokens % rows == 0:
            return rows
    return tokens


def lane_head(width):
    return lax.broadcasted_iota(jnp.int32, (1, width), 1) // HD


def attend_kernel(q_ref, k_ref, v_ref, o_ref, lse_ref, ext_ref):
    width = q_ref.shape[-1]
    seq = ext_ref.shape[0]

    @pl.when((pl.program_id(0) == 0) & (pl.program_id(1) == 0))
    def _():
        ext_ref[:, :width] = v_ref[:, 0].reshape(seq, width)
        ext_ref[:, width:] = jnp.ones((seq, ext_ref.shape[1] - width), BF16)

    queries = q_ref[0, 0] * SCALE
    keys = k_ref[:, 0].reshape(seq, width)
    lane = lane_head(width)
    mixed = jnp.zeros(queries.shape, F32)
    logs = jnp.zeros(queries.shape, F32)
    for head in range(width // HD):
        own = lane == head
        scores = times_transposed(jnp.where(own, queries, 0).astype(BF16), keys)
        row_max = jnp.max(scores, axis=1, keepdims=True)
        weight = jnp.exp(scores - row_max).astype(BF16)
        total = matmul(weight, ext_ref[...])
        row_total = total[:, width : 2 * width]
        mixed = jnp.where(own, total[:, :width] / row_total, mixed)
        logs = jnp.where(own, row_max + jnp.log(row_total), logs)
    o_ref[0] = mixed.astype(BF16)
    lse_ref[0] = logs


def attend(packed):
    parts, _, tokens, width = packed.shape
    rows = block_rows(tokens)
    return pl.pallas_call(
        attend_kernel,
        name="attend",
        grid=(parts, tokens // rows),
        in_specs=[
            pl.BlockSpec((1, 1, rows, width), lambda i, j: (i, 0, j, 0)),
            pl.BlockSpec((parts, 1, tokens, width), lambda i, j: (0, 1, 0, 0)),
            pl.BlockSpec((parts, 1, tokens, width), lambda i, j: (0, 2, 0, 0)),
        ],
        out_specs=[
            pl.BlockSpec((1, rows, width), lambda i, j: (i, j, 0)),
            pl.BlockSpec((1, rows, width), lambda i, j: (i, j, 0)),
        ],
        out_shape=[
            jax.ShapeDtypeStruct((parts, tokens, width), BF16),
            jax.ShapeDtypeStruct((parts, tokens, width), F32),
        ],
        scratch_shapes=[pltpu.VMEM((parts * tokens, 2 * width), BF16)],
        cost_estimate=pl.CostEstimate(
            flops=2 * 512 * width // HD * (parts * tokens) ** 2,
            transcendentals=width // HD * (parts * tokens) ** 2,
            bytes_accessed=12 * parts * tokens * width,
        ),
        compiler_params=pltpu.CompilerParams(vmem_limit_bytes=VMEM_BYTES),
    )(packed, packed, packed)


def attend_back_kernel(q_ref, k_ref, v_ref, o_ref, g_ref, lse_ref, out_ref, dk_ref, dv_ref):
    part, block = pl.program_id(0), pl.program_id(1)
    parts, tokens = k_ref.shape[0], k_ref.shape[2]
    rows, width = q_ref.shape[2], q_ref.shape[3]
    seq = parts * tokens

    @pl.when((part == 0) & (block == 0))
    def _():
        dk_ref[...] = jnp.zeros_like(dk_ref)
        dv_ref[...] = jnp.zeros_like(dv_ref)

    queries = q_ref[0, 0] * SCALE
    grads = g_ref[0]
    keys = k_ref[:, 0].reshape(seq, width)
    values = v_ref[:, 0].reshape(seq, width)
    product = grads.astype(F32) * o_ref[0].astype(F32)
    logs = lse_ref[0]
    query_rows = queries.T
    grad_rows = grads.T
    lane = lane_head(width)
    dquery = jnp.zeros((rows, width), F32)
    for head in range(width // HD):
        own = lane == head
        span = slice(head * HD, (head + 1) * HD)
        scores = times_transposed(jnp.where(own, queries, 0).astype(BF16), keys)
        weight = jnp.exp(scores - logs[:, head * HD : head * HD + 1])
        inner = jnp.sum(jnp.where(own, product, 0.0), axis=1, keepdims=True)
        weight_grad = times_transposed(jnp.where(own, grads, 0).astype(BF16), values)
        score_grad = (weight * (weight_grad - inner)).astype(BF16)
        dv_ref[span, :] += matmul(grad_rows[span], weight.astype(BF16))
        dk_ref[span, :] += matmul(query_rows[span], score_grad)
        dquery = jnp.where(own, matmul(score_grad, keys), dquery)
    out_ref[part, 0, pl.ds(pl.multiple_of(block * rows, rows), rows), :] = (dquery * SCALE).astype(BF16)

    @pl.when((part == parts - 1) & (block == pl.num_programs(1) - 1))
    def _():
        out_ref[:, 1] = dk_ref[...].T.astype(BF16).reshape(parts, tokens, width)
        out_ref[:, 2] = dv_ref[...].T.astype(BF16).reshape(parts, tokens, width)


def attend_back(packed, mixed, grads, logs):
    parts, _, tokens, width = packed.shape
    rows = block_rows(tokens)
    own = pl.BlockSpec((1, rows, width), lambda i, j: (i, j, 0))
    return pl.pallas_call(
        attend_back_kernel,
        name="attend_back",
        grid=(parts, tokens // rows),
        in_specs=[
            pl.BlockSpec((1, 1, rows, width), lambda i, j: (i, 0, j, 0)),
            pl.BlockSpec((parts, 1, tokens, width), lambda i, j: (0, 1, 0, 0)),
            pl.BlockSpec((parts, 1, tokens, width), lambda i, j: (0, 2, 0, 0)),
            own,
            own,
            own,
        ],
        out_specs=pl.BlockSpec((parts, 3, tokens, width), lambda i, j: (0, 0, 0, 0)),
        out_shape=jax.ShapeDtypeStruct((parts, 3, tokens, width), BF16),
        scratch_shapes=[
            pltpu.VMEM((width, parts * tokens), F32),
            pltpu.VMEM((width, parts * tokens), F32),
        ],
        cost_estimate=pl.CostEstimate(
            flops=5 * 512 * width // HD * (parts * tokens) ** 2,
            transcendentals=width // HD * (parts * tokens) ** 2,
            bytes_accessed=20 * parts * tokens * width,
        ),
        compiler_params=pltpu.CompilerParams(vmem_limit_bytes=VMEM_BYTES),
    )(packed, packed, packed, mixed, grads, logs)


def xor_order(pieces, index):
    count = pieces.shape[0]
    bit = 1
    while bit < count:
        split = pieces.reshape((count // (2 * bit), 2, bit) + pieces.shape[1:])
        pieces = jnp.where((index & bit) != 0, split[:, ::-1], split).reshape(pieces.shape)
        bit *= 2
    return pieces


def exchange(pieces):
    count = pieces.shape[0]
    return jnp.stack(
        [pieces[0]]
        + [lax.ppermute(pieces[k], "z", [(i, i ^ k) for i in range(count)]) for k in range(1, count)]
    )


def swap(value):
    return lax.ppermute(value, "c", [(0, 1), (1, 0)])


def with_partner(rows):
    return jnp.concatenate([rows, swap(rows)], axis=0)


def sum_with_partner(partial_rows):
    half = partial_rows.shape[0] // 2
    return partial_rows[:half] + swap(partial_rows[half:])


def add_rounded(left, right):
    return (left.astype(F32) + right.astype(F32)).astype(left.dtype)


def merge(pieces):
    blocks = [piece[:, start : start + LANES] for piece in pieces for start in range(0, piece.shape[1], LANES)]
    return jnp.concatenate([block.astype(BF16) for block in blocks], axis=0)


def join_kernel(core_ref, *refs, moves, count):
    out_ref = refs[-1]
    for layer in range(out_ref.shape[0]):
        blocks = refs[2 * count * layer : 2 * count * (layer + 1)]
        for half, source, target, size in moves:
            mine = core_ref[0] == (pl.program_id(0) if half is None else half)
            place, start = source // LANES, source % LANES
            span = slice(start, start + size)
            part = jnp.where(mine, blocks[place][:, span], blocks[count + place][:, span])
            out_ref[layer, :, target : target + size] = part.astype(F32)


def join(pairs, core, rows, columns, offsets, moves, by_rows):
    count = columns // LANES
    block = next(size for size in (64, 32, 16, 8) if rows % size == 0)
    steps = rows // block
    specs, operands = [], []
    for pair, offset in zip(pairs, offsets):
        for member in pair:
            for place in range(count):
                first = offset // block + place * steps
                specs.append(pl.BlockSpec((block, LANES), lambda h, i, core, first=first: (first + i, 0)))
                operands.append(member)
    if by_rows:
        grid, shape = (2, steps), (len(pairs), 2 * rows, columns)
    else:
        grid, shape = (1, steps), (len(pairs), rows, 2 * columns)
    return pl.pallas_call(
        partial(join_kernel, moves=moves, count=count),
        name="join",
        grid_spec=pltpu.PrefetchScalarGridSpec(
            num_scalar_prefetch=1,
            grid=grid,
            in_specs=specs,
            out_specs=pl.BlockSpec((len(pairs), block, shape[2]), lambda h, i, core: (0, h * steps + i, 0)),
        ),
        out_shape=jax.ShapeDtypeStruct(shape, F32),
        compiler_params=pltpu.CompilerParams(vmem_limit_bytes=VMEM_BYTES),
    )(core, *operands)


class Pipeline:
    def __init__(self):
        self.running = []
        self.finished = {}
        self.fresh = {}

    def add(self, flow, finish):
        self.running.append([flow, finish, None, ""])

    def advance(self, main, point=None, last=False):
        due = []
        for item in self.running:
            if isinstance(item[3], int):
                item[3] -= 1
            if item[2] is None or last or item[3] == 0 or item[3] == point:
                due.append(item)
        flights = [item[2] for item in due]
        main, flights, fresh = lax.optimization_barrier((main, flights, self.fresh))
        self.finished.update(fresh)
        self.fresh = {}
        steps = []
        waiting = list(zip(due, flights))
        while waiting:
            item, flight = waiting.pop(0)
            try:
                steps.append((item,) + item[0].send(flight))
            except StopIteration as stop:
                self.running.remove(item)
                known = len(self.running)
                item[1](stop.value)
                waiting += [(added, None) for added in self.running[known:]]
        sends = [step[1] for step in steps]
        main, sends = lax.optimization_barrier((main, sends))
        for (item, _, start, hold), values in zip(steps, sends):
            item[2], item[3] = start(values), hold
        return main

    def drain(self):
        while self.running:
            self.advance((), last=True)
        self.finished.update(self.fresh)


def bit_count(number):
    return number.bit_length() - 1


def swap_pairs(count, bit):
    return [(i, i ^ (1 << bit)) for i in range(count)]


def pick(values, place, axis):
    return lax.dynamic_index_in_dim(values, place, axis, keepdims=False)


def pause(point):
    yield [], lambda values: [], point


def scatter_flow(gradient, index, count, points):
    bits = bit_count(count)
    half = gradient.shape[1] // 2
    lead = (2,) * bits + (gradient.shape[0] // count,)
    halves = [gradient[:, :half].reshape(lead + (half,)), gradient[:, half:].reshape(lead + (half,))]
    for step in range(bits):
        places = [(bits - 1 - step, 0), (step, bits - 1 - step)]
        mine = [(index >> bit) & 1 for bit, _ in places]
        sends = [pick(value, 1 - own, axis) for value, own, (_, axis) in zip(halves, mine, places)]
        kept = [pick(value, own, axis) for value, own, (_, axis) in zip(halves, mine, places)]

        def start(values, places=places):
            return [
                lax.ppermute(value, "shard", swap_pairs(count, bit)) for value, (bit, _) in zip(values, places)
            ]

        arrived = yield sends, start, points[min(step, len(points) - 1)]
        halves = [add_rounded(own, other) for own, other in zip(kept, arrived)]
    return jnp.concatenate(halves, axis=1)


def offload_flow(gradient, point):
    def start(values):
        return [lax.psum_scatter(values[0], "shard", scatter_dimension=0, tiled=True)]

    (piece,) = yield [gradient], start, point
    return piece


def line_flow(piece, count, points):
    total, carry = piece.astype(F32), None
    for step in range(1, count):
        begin, point = points[step - 1] if step <= len(points) else ("", 1)
        if begin:
            yield from pause(begin)
        pairs = [(step - 1, step), (count - step, count - step - 1)]
        send = piece if carry is None else add_rounded(piece, carry)

        def start(values, pairs=pairs):
            return [lax.ppermute(values[0], "z", pairs)]

        (carry,) = yield [send], start, point
        total = total + carry.astype(F32)
    return total.astype(piece.dtype)


def halving_flow(values, index, count):
    bits = bit_count(count)
    for bit in range(bits):
        upper = (index >> bit) & 1
        halves = values.reshape((2, values.shape[0] // 2) + values.shape[1:])

        def start(sent, bit=bit):
            return [lax.ppermute(sent[0], "z", swap_pairs(count, bit))]

        (other,) = yield [pick(halves, 1 - upper, 0)], start, 1
        values = add_rounded(pick(halves, upper, 0), other)
    for bit in reversed(range(bits)):
        upper = ((index >> bit) & 1) == 1

        def start(sent, bit=bit):
            return [lax.ppermute(sent[0], "z", swap_pairs(count, bit))]

        (other,) = yield [values], start, 1
        values = jnp.concatenate([jnp.where(upper, other, values), jnp.where(upper, values, other)], axis=0)
    return values


def gather_flow(part, index, count, holds):
    bits = bit_count(count)
    half = part.shape[1] // 2
    halves = [part[:, :half], part[:, half:]]
    for step in range(bits):
        places = [(step, 0), (bits - 1 - step, step)]

        def start(values, places=places):
            return [
                lax.ppermute(value, "shard", swap_pairs(count, bit)) for value, (bit, _) in zip(values, places)
            ]

        arrived = yield halves, start, holds[min(step, len(holds) - 1)]
        for place, (bit, axis) in enumerate(places):
            upper, own, other = ((index >> bit) & 1) == 1, halves[place], arrived[place]
            halves[place] = jnp.stack([jnp.where(upper, other, own), jnp.where(upper, own, other)], axis=axis)
    return jnp.concatenate([value.reshape(-1, half) for value in halves], axis=1)


def gelu_parts(pre_act):
    cdf = 0.5 * (1.0 + lax.erf(pre_act * (0.5**0.5)))
    density = jnp.exp(-0.5 * pre_act * pre_act) * 0.3989422804014327
    return (pre_act * cdf).astype(BF16), (cdf + pre_act * density).astype(BF16)


def body(
    images,
    norm1_scale,
    norm1_shift,
    qkv_weight,
    qv_bias,
    out_weight,
    out_bias,
    norm2_scale,
    norm2_shift,
    up_weight,
    up_bias,
    down_weight,
    down_bias,
    cotangent,
):
    image_count, local_len, width = images.shape
    z_count = lax.axis_size("z")
    shards = lax.axis_size("shard")
    z_index, c_index, s_index = lax.axis_index("z"), lax.axis_index("c"), lax.axis_index("shard")
    layers = norm1_scale.shape[0]
    hidden_units = up_bias.shape[1] * shards
    half_width = width // 2
    group = half_width // z_count
    tokens = 2 * local_len

    def my_half(values, axis):
        return lax.dynamic_index_in_dim(values, c_index, axis, keepdims=False)

    def gather(values):
        return lax.all_gather(values, "shard", axis=0, tiled=True)

    vectors = (norm1_scale, norm1_shift, out_bias, norm2_scale, norm2_shift, down_bias, qv_bias, up_bias)
    sizes = [member.shape[1] for member in vectors]
    offsets = [sum(sizes[:place]) for place in range(len(sizes) + 1)]
    vectors_full = lax.all_gather(jnp.concatenate(vectors, axis=1), "shard", axis=0)

    def full_vector(layer, place):
        return vectors_full[:, layer, offsets[place] : offsets[place + 1]].reshape(-1).astype(F32)

    pipeline = Pipeline()
    weights = []
    for layer in range(layers):
        qkv_part = my_half(qkv_weight[layer].reshape(-1, 3, shards, 2, half_width // shards), 3)
        qkv_part = jnp.swapaxes(qkv_part.reshape(-1, 3, z_count, group), 1, 2).reshape(-1, 3 * half_width)
        up_part = my_half(up_weight[layer].reshape(-1, shards, 2, hidden_units // 2 // shards), 2)
        held = {
            "out_part": my_half(out_weight[layer].reshape(2, -1, width), 0),
            "up": gather(up_part.reshape(-1, hidden_units // 2)),
            "down": gather(my_half(down_weight[layer].reshape(2, -1, width), 0)),
        }
        if layer == 0:
            held["qkv"] = gather(qkv_part)
        else:
            held["qkv_part"] = qkv_part
        weights.append(held)

    def fetch(layer, name, holds=(1,)):
        def finish(full):
            weights[layer][name] = full

        pipeline.add(gather_flow(weights[layer][name + "_part"], s_index, shards, holds), finish)

    stream = images.astype(F32).reshape(-1, width)
    saved = []
    for layer in range(layers):
        held = weights[layer]
        scale_one, shift_one, out_shift, scale_two, shift_two, down_shift, qv_full, up_all = [
            full_vector(layer, place) for place in range(8)
        ]
        qv_halves = my_half(qv_full.reshape(2, shards, 2, half_width // shards), 2).reshape(2, z_count, group)
        qkv_shift = jnp.stack([qv_halves[0], jnp.zeros_like(qv_halves[0]), qv_halves[1]], axis=1).reshape(-1)
        up_shift = my_half(up_all.reshape(shards, 2, -1), 1).reshape(-1)

        if layer == 0:
            fetch(layer, "out")
        normed_own, average_one, inverse_one = norm_forward(stream, scale_one, shift_one)
        normed_own = pipeline.advance(normed_own)
        normed_one = with_partner(normed_own)
        projected = (matmul(normed_one, held["qkv"]) + qkv_shift).astype(BF16)
        pieces = projected.reshape(tokens, z_count, 3, group).transpose(1, 2, 0, 3)
        if layer + 1 < layers:
            fetch(layer + 1, "qkv")
        pieces = pipeline.advance(xor_order(pieces, z_index))
        packed = pipeline.advance(exchange(pieces))
        mixed, logs = attend(packed)
        mixed = pipeline.advance(mixed)
        while "out" not in held:
            mixed = pipeline.advance(mixed)
        attended = xor_order(exchange(mixed), z_index).transpose(1, 0, 2).reshape(tokens, half_width)
        middle = stream + sum_with_partner(matmul(attended, held["out"])) + out_shift
        if layer + 1 < layers:
            fetch(layer + 1, "out", (1, 3))
        middle = pipeline.advance(middle)
        two_own, average_two, inverse_two = norm_forward(middle, scale_two, shift_two)
        normed_two = with_partner(two_own)
        pre_act = matmul(normed_two, held["up"]) + up_shift
        hidden, slope = gelu_parts(pre_act)
        saved.append(
            (
                stream,
                average_one,
                inverse_one,
                normed_one,
                packed,
                mixed,
                logs,
                attended,
                middle,
                average_two,
                inverse_two,
                normed_two,
                hidden,
                slope,
                scale_one,
                scale_two,
            )
        )
        stream = middle + sum_with_partner(matmul(hidden, held["down"])) + down_shift
        stream = pipeline.advance(stream)
        while layer + 1 < layers and "qkv" not in weights[layer + 1]:
            stream = pipeline.advance(stream)
    results = stream.astype(BF16).reshape(image_count, local_len, width)

    core = c_index.astype(jnp.int32).reshape(1)
    block = half_width // shards
    cut = min(block, group)
    qkv_moves = []
    for part in range(3):
        for start in range(0, half_width, cut):
            source = start // group * 3 * group + part * group + start % group
            target = part * width + start // block * 2 * block + start % block
            qkv_moves += [(core_of, source, target + core_of * block, cut) for core_of in range(2)]
    block_up = hidden_units // 2 // shards
    up_moves = [
        (core_of, place * block_up, (2 * place + core_of) * block_up, block_up)
        for place in range(shards)
        for core_of in range(2)
    ]
    row_moves = [(None, start, start, LANES) for start in range(0, width, LANES)]
    local = width // shards
    forms = {
        "down": (hidden_units // 2 // shards, width, row_moves, True),
        "up": (local, hidden_units // 2, up_moves, False),
        "out": (half_width // shards, width, row_moves, True),
        "qkv": (local, 3 * half_width, qkv_moves, False),
    }
    small_rows = 64
    groups = [
        [("down",), ("up",)] + ([("out", "qkv"), ("small",)] if layer == 0 else [("out", "qkv", "small")])
        for layer in range(layers)
    ]

    def line_points(layer, name):
        if layer == 0:
            return {"down": [("", "q0"), ("", "end0")], "up": [("", "end0")]}.get(name, [])
        end, q, later = f"end{layer}", f"q{layer - 1}", f"end{layer - 1}"
        b, c, d, e = [f"{kind}{layer - 1}" for kind in "bcde"]
        return {
            "down": [("", end), ("", b), (c, d)],
            "up": [("", b), (c, d), (e, q)],
            "out": [("", d), (e, q), ("", later)],
        }[name]

    pieces_of = [{} for _ in range(layers)]
    sums_of = [{} for _ in range(layers)]

    def total_flow(merged, points, halving):
        if halving:
            merged = yield from halving_flow(merged, z_index, z_count)
        else:
            merged = yield from line_flow(merged, z_count, points)
        (other,) = yield [merged], lambda values: [swap(values[0])], 1
        return merged, other

    def arrived_in(layer, name, piece):
        pieces_of[layer][name] = piece
        for names in groups[layer]:
            if name in names and all(member in pieces_of[layer] for member in names):
                members = [pieces_of[layer][member] for member in names]
                flow = total_flow(merge(members), line_points(layer, names[0]), layer == 0 and "qkv" in names)
                pipeline.add(flow, partial(summed, layer, names, [member.size // LANES for member in members]))

    def summed(layer, names, extents, pair):
        offset = 0
        for name, extent in zip(names, extents):
            sums_of[layer][name] = (pair, offset)
            offset += extent
            if all(name in sums for sums in sums_of):
                pairs = [sums[name][0] for sums in sums_of]
                starts = [sums[name][1] for sums in sums_of]
                if name == "small":
                    count = offsets[-1] // LANES
                    pipeline.fresh[name] = jnp.stack(
                        [
                            sum(member[start : start + count].astype(F32) for member in pair).reshape(-1)
                            for pair, start in zip(pairs, starts)
                        ]
                    )
                else:
                    rows, columns, moves, by_rows = forms[name]
                    pipeline.fresh[name] = join(pairs, core, rows, columns, starts, moves, by_rows)

    def reduce_weight(layer, name, gradient, points):
        if name != "small":
            gradient = gradient.astype(BF16)
        if isinstance(points, tuple):
            flow = scatter_flow(gradient, s_index, shards, points)
        else:
            flow = offload_flow(gradient, points)
        pipeline.add(flow, partial(arrived_in, layer, name))

    grad_stream = cotangent.astype(F32).reshape(-1, width)
    for layer in reversed(range(layers)):
        (
            stream_in,
            average_one,
            inverse_one,
            normed_one,
            packed,
            mixed,
            logs,
            attended,
            middle,
            average_two,
            inverse_two,
            normed_two,
            hidden,
            slope,
            scale_one,
            scale_two,
        ) = saved[layer]
        held = weights[layer]
        late = layer == 0
        branch_own = grad_stream.astype(BF16)
        branch_grad = with_partner(branch_own)
        grad_down_b = jnp.sum(branch_own.astype(F32), axis=0)
        if not late:
            reduce_weight(layer, "down", outer_sum(hidden, branch_grad), f"e{layer}")
        pre_grad = (times_transposed(branch_grad, held["down"]) * slope.astype(F32)).astype(BF16)
        two_grad = sum_with_partner(times_transposed(pre_grad, held["up"]))
        grad_up_b = jnp.sum(pre_grad.astype(F32), axis=0)
        middle_back, grad_scale_two, grad_shift_two = norm_backward(
            middle, average_two, inverse_two, scale_two, two_grad
        )
        middle_grad = grad_stream + middle_back
        out_own = middle_grad.astype(BF16)
        out_grad = with_partner(out_own)
        grad_out_b = jnp.sum(out_own.astype(F32), axis=0)
        attended_grad = times_transposed(out_grad, held["out"]).astype(BF16)
        grad_pieces = attended_grad.reshape(tokens, z_count, group).transpose(1, 0, 2)
        grad_pieces = pipeline.advance(xor_order(grad_pieces, z_index), f"b{layer}")
        head_grad = exchange(grad_pieces)
        reduce_weight(layer, "up", outer_sum(normed_two, pre_grad), f"q{layer}" if late else f"end{layer}")
        if late:
            reduce_weight(layer, "down", outer_sum(hidden, branch_grad), (f"d{layer}", f"e{layer}"))
        head_grad = pipeline.advance(head_grad, f"c{layer}")
        heads_back = pipeline.advance(attend_back(packed, mixed, head_grad, logs), f"d{layer}")
        reduce_weight(layer, "out", outer_sum(attended, out_grad), f"end{layer}" if late else f"c{layer - 1}")
        arrived = pipeline.advance(exchange(heads_back), f"e{layer}")
        projected_grad = xor_order(arrived, z_index).transpose(2, 0, 1, 3)
        projected_grad = projected_grad.reshape(tokens, 3 * half_width)
        qkv_points = (f"end{layer}", 1) if late else f"c{layer - 1}"
        reduce_weight(layer, "qkv", outer_sum(normed_one, projected_grad), qkv_points)
        if late:
            projected_grad = pipeline.advance(projected_grad, f"q{layer}")
        one_grad = sum_with_partner(times_transposed(projected_grad, held["qkv"]))
        column_sums = jnp.sum(projected_grad.astype(F32), axis=0).reshape(z_count, 3, group)
        grad_qv_b = jnp.stack([column_sums[:, 0], column_sums[:, 2]])
        stream_back, grad_scale_one, grad_shift_one = norm_backward(
            stream_in, average_one, inverse_one, scale_one, one_grad
        )
        grad_stream = middle_grad + stream_back

        def spread(values, lead):
            values = values.reshape(lead, shards, 1, -1)
            nothing = jnp.zeros_like(values)
            halves = jnp.concatenate(
                [
                    jnp.where(c_index == 0, values, nothing),
                    jnp.where(c_index == 0, nothing, values),
                ],
                axis=2,
            )
            return halves.reshape(shards, -1)

        small = jnp.concatenate(
            [
                member.reshape(shards, -1)
                for member in (
                    grad_scale_one,
                    grad_shift_one,
                    grad_out_b,
                    grad_scale_two,
                    grad_shift_two,
                    grad_down_b,
                    spread(grad_qv_b, 2),
                    spread(grad_up_b, 1),
                )
            ],
            axis=1,
        )
        small = jnp.pad(small.reshape(shards, -1, LANES), ((0, 0), (0, small_rows - offsets[-1] // LANES), (0, 0)))
        reduce_weight(layer, "small", small.reshape(-1, LANES), 1 if late else f"c{layer - 1}")
        grad_stream = pipeline.advance(grad_stream, f"end{layer}")

    pipeline.drain()
    sums = pipeline.finished
    vector_grads = [sums["small"][:, offsets[place] : offsets[place + 1]] for place in range(8)]
    grad_qkv, grad_out, grad_up, grad_down = sums["qkv"], sums["out"], sums["up"], sums["down"]
    input_grad = grad_stream.reshape(image_count, local_len, width)
    return (
        results,
        input_grad,
        vector_grads[0],
        vector_grads[1],
        grad_qkv,
        vector_grads[6],
        grad_out,
        vector_grads[2],
        vector_grads[3],
        vector_grads[4],
        grad_up,
        vector_grads[7],
        grad_down,
        vector_grads[5],
    )


def solution(mesh):
    seq, shards = mesh.devices.shape
    cores = Mesh(mesh.devices.reshape(seq // 2, 2, shards), ("z", "c", "shard"))
    rows = P("shard", ("z", "c"), None)
    vector = P(None, "shard")
    matrix = P(None, "shard", None)
    parameters = (
        vector,
        vector,
        matrix,
        vector,
        matrix,
        vector,
        vector,
        vector,
        matrix,
        vector,
        matrix,
        vector,
    )
    return jax.shard_map(
        body,
        mesh=cores,
        in_specs=(rows,) + parameters + (rows,),
        out_specs=(rows, rows) + parameters,
        check_vma=False,
    )
```

```python
from functools import partial

import jax
import jax.numpy as jnp
from jax import lax
from jax.experimental import pallas as pl
from jax.experimental.pallas import tpu as pltpu
from jax.sharding import Mesh
from jax.sharding import PartitionSpec as P

HD = 64
SCALE = HD ** (-0.5)
F32 = jnp.float32
BF16 = jnp.bfloat16
LANES = 512
VMEM_BYTES = 56 * 1024 * 1024


def matmul(left, right):
    return jnp.dot(left, right, preferred_element_type=F32)


def outer_sum(left, right):
    return lax.dot_general(left, right, (((0,), (0,)), ((), ())), preferred_element_type=F32)


def times_transposed(left, right):
    return lax.dot_general(left, right, (((1,), (1,)), ((), ())), preferred_element_type=F32)


def norm_forward(stream, scales, offset):
    average = jnp.mean(stream, axis=-1, keepdims=True)
    centered = stream - average
    variance = jnp.mean(centered * centered, axis=-1, keepdims=True)
    inverse = lax.rsqrt(variance + 1e-06)
    return (centered * inverse * scales + offset).astype(BF16), average, inverse


def norm_backward(stream, average, inverse, scales, upstream):
    unit_rows = (stream - average) * inverse
    grad_scale = jnp.sum(upstream * unit_rows, axis=0)
    grad_shift = jnp.sum(upstream, axis=0)
    scaled_grad = upstream * scales
    stream_grad = inverse * (
        scaled_grad
        - jnp.mean(scaled_grad, axis=-1, keepdims=True)
        - unit_rows * jnp.mean(scaled_grad * unit_rows, axis=-1, keepdims=True)
    )
    return stream_grad, grad_scale, grad_shift


def block_rows(tokens):
    for rows in (576, 288, 192, 144, 96, 48, 16):
        if tokens % rows == 0:
            return rows
    return tokens


def lane_head(width):
    return lax.broadcasted_iota(jnp.int32, (1, width), 1) // HD


def attend_kernel(q_ref, k_ref, v_ref, o_ref, lse_ref, ext_ref):
    width = q_ref.shape[-1]
    seq = ext_ref.shape[0]

    @pl.when((pl.program_id(0) == 0) & (pl.program_id(1) == 0))
    def _():
        ext_ref[:, :width] = v_ref[:, 0].reshape(seq, width)
        ext_ref[:, width:] = jnp.ones((seq, ext_ref.shape[1] - width), BF16)

    queries = q_ref[0, 0] * SCALE
    keys = k_ref[:, 0].reshape(seq, width)
    lane = lane_head(width)
    mixed = jnp.zeros(queries.shape, F32)
    logs = jnp.zeros(queries.shape, F32)
    for head in range(width // HD):
        own = lane == head
        scores = times_transposed(jnp.where(own, queries, 0).astype(BF16), keys)
        row_max = jnp.max(scores, axis=1, keepdims=True)
        weight = jnp.exp(scores - row_max).astype(BF16)
        total = matmul(weight, ext_ref[...])
        row_total = total[:, width : 2 * width]
        mixed = jnp.where(own, total[:, :width] / row_total, mixed)
        logs = jnp.where(own, row_max + jnp.log(row_total), logs)
    o_ref[0] = mixed.astype(BF16)
    lse_ref[0] = logs


def attend(packed):
    parts, _, tokens, width = packed.shape
    rows = block_rows(tokens)
    return pl.pallas_call(
        attend_kernel,
        name="attend",
        grid=(parts, tokens // rows),
        in_specs=[
            pl.BlockSpec((1, 1, rows, width), lambda i, j: (i, 0, j, 0)),
            pl.BlockSpec((parts, 1, tokens, width), lambda i, j: (0, 1, 0, 0)),
            pl.BlockSpec((parts, 1, tokens, width), lambda i, j: (0, 2, 0, 0)),
        ],
        out_specs=[
            pl.BlockSpec((1, rows, width), lambda i, j: (i, j, 0)),
            pl.BlockSpec((1, rows, width), lambda i, j: (i, j, 0)),
        ],
        out_shape=[
            jax.ShapeDtypeStruct((parts, tokens, width), BF16),
            jax.ShapeDtypeStruct((parts, tokens, width), F32),
        ],
        scratch_shapes=[pltpu.VMEM((parts * tokens, 2 * width), BF16)],
        cost_estimate=pl.CostEstimate(
            flops=2 * 512 * width // HD * (parts * tokens) ** 2,
            transcendentals=width // HD * (parts * tokens) ** 2,
            bytes_accessed=12 * parts * tokens * width,
        ),
        compiler_params=pltpu.CompilerParams(vmem_limit_bytes=VMEM_BYTES),
    )(packed, packed, packed)


def attend_back_kernel(q_ref, k_ref, v_ref, o_ref, g_ref, lse_ref, out_ref, dk_ref, dv_ref):
    part, block = pl.program_id(0), pl.program_id(1)
    parts, tokens = k_ref.shape[0], k_ref.shape[2]
    rows, width = q_ref.shape[2], q_ref.shape[3]
    seq = parts * tokens

    @pl.when((part == 0) & (block == 0))
    def _():
        dk_ref[...] = jnp.zeros_like(dk_ref)
        dv_ref[...] = jnp.zeros_like(dv_ref)

    queries = q_ref[0, 0] * SCALE
    grads = g_ref[0]
    keys = k_ref[:, 0].reshape(seq, width)
    values = v_ref[:, 0].reshape(seq, width)
    product = grads.astype(F32) * o_ref[0].astype(F32)
    logs = lse_ref[0]
    query_rows = queries.T
    grad_rows = grads.T
    lane = lane_head(width)
    dquery = jnp.zeros((rows, width), F32)
    for head in range(width // HD):
        own = lane == head
        span = slice(head * HD, (head + 1) * HD)
        scores = times_transposed(jnp.where(own, queries, 0).astype(BF16), keys)
        weight = jnp.exp(scores - logs[:, head * HD : head * HD + 1])
        inner = jnp.sum(jnp.where(own, product, 0.0), axis=1, keepdims=True)
        weight_grad = times_transposed(jnp.where(own, grads, 0).astype(BF16), values)
        score_grad = (weight * (weight_grad - inner)).astype(BF16)
        dv_ref[span, :] += matmul(grad_rows[span], weight.astype(BF16))
        dk_ref[span, :] += matmul(query_rows[span], score_grad)
        dquery = jnp.where(own, matmul(score_grad, keys), dquery)
    out_ref[part, 0, pl.ds(pl.multiple_of(block * rows, rows), rows), :] = (dquery * SCALE).astype(BF16)

    @pl.when((part == parts - 1) & (block == pl.num_programs(1) - 1))
    def _():
        out_ref[:, 1] = dk_ref[...].T.astype(BF16).reshape(parts, tokens, width)
        out_ref[:, 2] = dv_ref[...].T.astype(BF16).reshape(parts, tokens, width)


def attend_back(packed, mixed, grads, logs):
    parts, _, tokens, width = packed.shape
    rows = block_rows(tokens)
    own = pl.BlockSpec((1, rows, width), lambda i, j: (i, j, 0))
    return pl.pallas_call(
        attend_back_kernel,
        name="attend_back",
        grid=(parts, tokens // rows),
        in_specs=[
            pl.BlockSpec((1, 1, rows, width), lambda i, j: (i, 0, j, 0)),
            pl.BlockSpec((parts, 1, tokens, width), lambda i, j: (0, 1, 0, 0)),
            pl.BlockSpec((parts, 1, tokens, width), lambda i, j: (0, 2, 0, 0)),
            own,
            own,
            own,
        ],
        out_specs=pl.BlockSpec((parts, 3, tokens, width), lambda i, j: (0, 0, 0, 0)),
        out_shape=jax.ShapeDtypeStruct((parts, 3, tokens, width), BF16),
        scratch_shapes=[
            pltpu.VMEM((width, parts * tokens), F32),
            pltpu.VMEM((width, parts * tokens), F32),
        ],
        cost_estimate=pl.CostEstimate(
            flops=5 * 512 * width // HD * (parts * tokens) ** 2,
            transcendentals=width // HD * (parts * tokens) ** 2,
            bytes_accessed=20 * parts * tokens * width,
        ),
        compiler_params=pltpu.CompilerParams(vmem_limit_bytes=VMEM_BYTES),
    )(packed, packed, packed, mixed, grads, logs)


def xor_order(pieces, index):
    count = pieces.shape[0]
    bit = 1
    while bit < count:
        split = pieces.reshape((count // (2 * bit), 2, bit) + pieces.shape[1:])
        pieces = jnp.where((index & bit) != 0, split[:, ::-1], split).reshape(pieces.shape)
        bit *= 2
    return pieces


def exchange(pieces):
    count = pieces.shape[0]
    return jnp.stack(
        [pieces[0]]
        + [lax.ppermute(pieces[k], "z", [(i, i ^ k) for i in range(count)]) for k in range(1, count)]
    )


def swap(value):
    return lax.ppermute(value, "c", [(0, 1), (1, 0)])


def with_partner(rows):
    return jnp.concatenate([rows, swap(rows)], axis=0)


def sum_with_partner(partial_rows):
    half = partial_rows.shape[0] // 2
    return partial_rows[:half] + swap(partial_rows[half:])


def add_rounded(left, right):
    return (left.astype(F32) + right.astype(F32)).astype(left.dtype)


def merge(pieces):
    blocks = [piece[:, start : start + LANES] for piece in pieces for start in range(0, piece.shape[1], LANES)]
    return jnp.concatenate([block.astype(BF16) for block in blocks], axis=0)


def join_kernel(core_ref, *refs, moves, count):
    out_ref = refs[-1]
    for layer in range(out_ref.shape[0]):
        blocks = refs[2 * count * layer : 2 * count * (layer + 1)]
        for half, source, target, size in moves:
            mine = core_ref[0] == (pl.program_id(0) if half is None else half)
            place, start = source // LANES, source % LANES
            span = slice(start, start + size)
            part = jnp.where(mine, blocks[place][:, span], blocks[count + place][:, span])
            out_ref[layer, :, target : target + size] = part.astype(F32)


def join(pairs, core, rows, columns, offsets, moves, by_rows):
    count = columns // LANES
    block = next(size for size in (64, 32, 16, 8) if rows % size == 0)
    steps = rows // block
    specs, operands = [], []
    for pair, offset in zip(pairs, offsets):
        for member in pair:
            for place in range(count):
                first = offset // block + place * steps
                specs.append(pl.BlockSpec((block, LANES), lambda h, i, core, first=first: (first + i, 0)))
                operands.append(member)
    if by_rows:
        grid, shape = (2, steps), (len(pairs), 2 * rows, columns)
    else:
        grid, shape = (1, steps), (len(pairs), rows, 2 * columns)
    return pl.pallas_call(
        partial(join_kernel, moves=moves, count=count),
        name="join",
        grid_spec=pltpu.PrefetchScalarGridSpec(
            num_scalar_prefetch=1,
            grid=grid,
            in_specs=specs,
            out_specs=pl.BlockSpec((len(pairs), block, shape[2]), lambda h, i, core: (0, h * steps + i, 0)),
        ),
        out_shape=jax.ShapeDtypeStruct(shape, F32),
        compiler_params=pltpu.CompilerParams(vmem_limit_bytes=VMEM_BYTES),
    )(core, *operands)


class Pipeline:
    def __init__(self, tied=True):
        self.tied = tied
        self.running = []
        self.finished = {}
        self.fresh = {}

    def add(self, flow, finish):
        self.running.append([flow, finish, None, ""])

    def advance(self, main, point=None, last=False):
        due = []
        for item in self.running:
            if isinstance(item[3], int):
                item[3] -= 1
            if item[2] is None or last or item[3] == 0 or item[3] == point:
                due.append(item)
        flights = [item[2] for item in due]
        fresh = self.fresh
        if self.tied:
            main, flights, fresh = lax.optimization_barrier((main, flights, fresh))
        self.finished.update(fresh)
        self.fresh = {}
        steps = []
        waiting = list(zip(due, flights))
        while waiting:
            item, flight = waiting.pop(0)
            try:
                steps.append((item,) + item[0].send(flight))
            except StopIteration as stop:
                self.running.remove(item)
                known = len(self.running)
                item[1](stop.value)
                waiting += [(added, None) for added in self.running[known:]]
        sends = [step[1] for step in steps]
        if self.tied:
            main, sends = lax.optimization_barrier((main, sends))
        for (item, _, start, hold), values in zip(steps, sends):
            item[2], item[3] = start(values), hold
        return main

    def drain(self):
        while self.running:
            self.advance((), last=True)
        self.finished.update(self.fresh)


def bit_count(number):
    return number.bit_length() - 1


def swap_pairs(count, bit):
    return [(i, i ^ (1 << bit)) for i in range(count)]


def pick(values, place, axis):
    return lax.dynamic_index_in_dim(values, place, axis, keepdims=False)


def pause(point):
    yield [], lambda values: [], point


def scatter_flow(gradient, index, count, points):
    bits = bit_count(count)
    half = gradient.shape[1] // 2
    lead = (2,) * bits + (gradient.shape[0] // count,)
    halves = [gradient[:, :half].reshape(lead + (half,)), gradient[:, half:].reshape(lead + (half,))]
    for step in range(bits):
        places = [(bits - 1 - step, 0), (step, bits - 1 - step)]
        mine = [(index >> bit) & 1 for bit, _ in places]
        sends = [pick(value, 1 - own, axis) for value, own, (_, axis) in zip(halves, mine, places)]
        kept = [pick(value, own, axis) for value, own, (_, axis) in zip(halves, mine, places)]

        def start(values, places=places):
            return [
                lax.ppermute(value, "shard", swap_pairs(count, bit)) for value, (bit, _) in zip(values, places)
            ]

        arrived = yield sends, start, points[min(step, len(points) - 1)]
        halves = [add_rounded(own, other) for own, other in zip(kept, arrived)]
    return jnp.concatenate(halves, axis=1)


def offload_flow(gradient, point):
    def start(values):
        return [lax.psum_scatter(values[0], "shard", scatter_dimension=0, tiled=True)]

    (piece,) = yield [gradient], start, point
    return piece


def line_flow(piece, count, points):
    total, carry = piece.astype(F32), None
    for step in range(1, count):
        begin, point = points[step - 1] if step <= len(points) else ("", 1)
        if begin:
            yield from pause(begin)
        pairs = [(step - 1, step), (count - step, count - step - 1)]
        send = piece if carry is None else add_rounded(piece, carry)

        def start(values, pairs=pairs):
            return [lax.ppermute(values[0], "z", pairs)]

        (carry,) = yield [send], start, point
        total = total + carry.astype(F32)
    return total.astype(piece.dtype)


def gather_flow(part, index, count, holds):
    bits = bit_count(count)
    half = part.shape[1] // 2
    halves = [part[:, :half], part[:, half:]]
    for step in range(bits):
        places = [(step, 0), (bits - 1 - step, step)]

        def start(values, places=places):
            return [
                lax.ppermute(value, "shard", swap_pairs(count, bit)) for value, (bit, _) in zip(values, places)
            ]

        arrived = yield halves, start, holds[min(step, len(holds) - 1)]
        for place, (bit, axis) in enumerate(places):
            upper, own, other = ((index >> bit) & 1) == 1, halves[place], arrived[place]
            halves[place] = jnp.stack([jnp.where(upper, other, own), jnp.where(upper, own, other)], axis=axis)
    return jnp.concatenate([value.reshape(-1, half) for value in halves], axis=1)


def gelu_parts(pre_act):
    cdf = 0.5 * (1.0 + lax.erf(pre_act * (0.5**0.5)))
    density = jnp.exp(-0.5 * pre_act * pre_act) * 0.3989422804014327
    return (pre_act * cdf).astype(BF16), (cdf + pre_act * density).astype(BF16)


def body(
    images,
    norm1_scale,
    norm1_shift,
    qkv_weight,
    qv_bias,
    out_weight,
    out_bias,
    norm2_scale,
    norm2_shift,
    up_weight,
    up_bias,
    down_weight,
    down_bias,
    cotangent,
):
    image_count, local_len, width = images.shape
    z_count = lax.axis_size("z")
    shards = lax.axis_size("shard")
    z_index, c_index, s_index = lax.axis_index("z"), lax.axis_index("c"), lax.axis_index("shard")
    layers = norm1_scale.shape[0]
    hidden_units = up_bias.shape[1] * shards
    half_width = width // 2
    group = half_width // z_count
    tokens = 2 * local_len

    def my_half(values, axis):
        return lax.dynamic_index_in_dim(values, c_index, axis, keepdims=False)

    def gather(values):
        return lax.all_gather(values, "shard", axis=0, tiled=True)

    vectors = (norm1_scale, norm1_shift, out_bias, norm2_scale, norm2_shift, down_bias, qv_bias, up_bias)
    sizes = [member.shape[1] for member in vectors]
    offsets = [sum(sizes[:place]) for place in range(len(sizes) + 1)]
    vectors_full = lax.all_gather(jnp.concatenate(vectors, axis=1), "shard", axis=0)

    def full_vector(layer, place):
        return vectors_full[:, layer, offsets[place] : offsets[place + 1]].reshape(-1).astype(F32)

    pipeline, free = Pipeline(), Pipeline(tied=False)
    weights = []
    for layer in range(layers):
        qkv_part = my_half(qkv_weight[layer].reshape(-1, 3, shards, 2, half_width // shards), 3)
        qkv_part = jnp.swapaxes(qkv_part.reshape(-1, 3, z_count, group), 1, 2).reshape(-1, 3 * half_width)
        up_part = my_half(up_weight[layer].reshape(-1, shards, 2, hidden_units // 2 // shards), 2)
        held = {
            "out_part": my_half(out_weight[layer].reshape(2, -1, width), 0),
            "up": gather(up_part.reshape(-1, hidden_units // 2)),
            "down": gather(my_half(down_weight[layer].reshape(2, -1, width), 0)),
        }
        if layer == 0:
            held["qkv"] = gather(qkv_part)
        else:
            held["qkv_part"] = qkv_part
        weights.append(held)

    def fetch(layer, name, holds=(1,)):
        def finish(full):
            weights[layer][name] = full

        pipeline.add(gather_flow(weights[layer][name + "_part"], s_index, shards, holds), finish)

    stream = images.astype(F32).reshape(-1, width)
    saved = []
    for layer in range(layers):
        held = weights[layer]
        scale_one, shift_one, out_shift, scale_two, shift_two, down_shift, qv_full, up_all = [
            full_vector(layer, place) for place in range(8)
        ]
        qv_halves = my_half(qv_full.reshape(2, shards, 2, half_width // shards), 2).reshape(2, z_count, group)
        qkv_shift = jnp.stack([qv_halves[0], jnp.zeros_like(qv_halves[0]), qv_halves[1]], axis=1).reshape(-1)
        up_shift = my_half(up_all.reshape(shards, 2, -1), 1).reshape(-1)

        if layer == 0:
            fetch(layer, "out")
        normed_own, average_one, inverse_one = norm_forward(stream, scale_one, shift_one)
        normed_own = pipeline.advance(normed_own)
        normed_one = with_partner(normed_own)
        projected = (matmul(normed_one, held["qkv"]) + qkv_shift).astype(BF16)
        pieces = projected.reshape(tokens, z_count, 3, group).transpose(1, 2, 0, 3)
        if layer + 1 < layers:
            fetch(layer + 1, "qkv")
        pieces = pipeline.advance(xor_order(pieces, z_index))
        packed = pipeline.advance(exchange(pieces))
        mixed, logs = attend(packed)
        mixed = pipeline.advance(mixed)
        while "out" not in held:
            mixed = pipeline.advance(mixed)
        attended = xor_order(exchange(mixed), z_index).transpose(1, 0, 2).reshape(tokens, half_width)
        middle = stream + sum_with_partner(matmul(attended, held["out"])) + out_shift
        if layer + 1 < layers:
            fetch(layer + 1, "out", (1, 3))
        middle = pipeline.advance(middle)
        two_own, average_two, inverse_two = norm_forward(middle, scale_two, shift_two)
        normed_two = with_partner(two_own)
        pre_act = matmul(normed_two, held["up"]) + up_shift
        hidden, slope = gelu_parts(pre_act)
        saved.append(
            (
                stream,
                average_one,
                inverse_one,
                normed_one,
                packed,
                mixed,
                logs,
                attended,
                middle,
                average_two,
                inverse_two,
                normed_two,
                hidden,
                slope,
                scale_one,
                scale_two,
            )
        )
        stream = middle + sum_with_partner(matmul(hidden, held["down"])) + down_shift
        stream = pipeline.advance(stream)
        while layer + 1 < layers and "qkv" not in weights[layer + 1]:
            stream = pipeline.advance(stream)
    results = stream.astype(BF16).reshape(image_count, local_len, width)

    core = c_index.astype(jnp.int32).reshape(1)
    block = half_width // shards
    cut = min(block, group)
    qkv_moves = []
    for part in range(3):
        for start in range(0, half_width, cut):
            source = start // group * 3 * group + part * group + start % group
            target = part * width + start // block * 2 * block + start % block
            qkv_moves += [(core_of, source, target + core_of * block, cut) for core_of in range(2)]
    block_up = hidden_units // 2 // shards
    up_moves = [
        (core_of, place * block_up, (2 * place + core_of) * block_up, block_up)
        for place in range(shards)
        for core_of in range(2)
    ]
    row_moves = [(None, start, start, LANES) for start in range(0, width, LANES)]
    local = width // shards
    forms = {
        "down": (hidden_units // 2 // shards, width, row_moves, True),
        "up": (local, hidden_units // 2, up_moves, False),
        "out": (half_width // shards, width, row_moves, True),
        "qkv": (local, 3 * half_width, qkv_moves, False),
    }
    small_rows = 64
    groups = [
        [("down",), ("up",)] + ([("out", "qkv"), ("small",)] if layer == 0 else [("out", "qkv", "small")])
        for layer in range(layers)
    ]

    def line_points(layer, name):
        if layer == 0:
            return [("", "end0")] if name == "down" else []
        end, later = f"end{layer}", f"end{layer - 1}"
        b, c, d, e = [f"{kind}{layer - 1}" for kind in "bcde"]
        return {
            "down": [("", end), ("", b), (c, d)],
            "up": [("", b), (c, d), (e, later)],
            "out": [("", d), (e, later)],
        }[name]

    pieces_of = [{} for _ in range(layers)]
    sums_of = [{} for _ in range(layers)]

    def total_flow(merged, points):
        merged = yield from line_flow(merged, z_count, points)
        (other,) = yield [merged], lambda values: [swap(values[0])], 1
        return merged, other

    def arrived_in(layer, name, piece):
        pieces_of[layer][name] = piece
        for names in groups[layer]:
            if name in names and all(member in pieces_of[layer] for member in names):
                members = [pieces_of[layer][member] for member in names]
                flow = total_flow(merge(members), line_points(layer, names[0]))
                line = free if layer == 0 and "qkv" in names else pipeline
                line.add(flow, partial(summed, layer, names, [member.size // LANES for member in members]))

    def summed(layer, names, extents, pair):
        offset = 0
        for name, extent in zip(names, extents):
            sums_of[layer][name] = (pair, offset)
            offset += extent
            if all(name in sums for sums in sums_of):
                pairs = [sums[name][0] for sums in sums_of]
                starts = [sums[name][1] for sums in sums_of]
                if name == "small":
                    count = offsets[-1] // LANES
                    pipeline.fresh[name] = jnp.stack(
                        [
                            sum(member[start : start + count].astype(F32) for member in pair).reshape(-1)
                            for pair, start in zip(pairs, starts)
                        ]
                    )
                else:
                    rows, columns, moves, by_rows = forms[name]
                    pipeline.fresh[name] = join(pairs, core, rows, columns, starts, moves, by_rows)

    def reduce_weight(layer, name, gradient, points):
        if name != "small":
            gradient = gradient.astype(BF16)
        if isinstance(points, tuple):
            flow = scatter_flow(gradient, s_index, shards, points)
        else:
            flow = offload_flow(gradient, points)
        line = free if layer == 0 and name == "qkv" else pipeline
        line.add(flow, partial(arrived_in, layer, name))

    grad_stream = cotangent.astype(F32).reshape(-1, width)
    for layer in reversed(range(layers)):
        (
            stream_in,
            average_one,
            inverse_one,
            normed_one,
            packed,
            mixed,
            logs,
            attended,
            middle,
            average_two,
            inverse_two,
            normed_two,
            hidden,
            slope,
            scale_one,
            scale_two,
        ) = saved[layer]
        held = weights[layer]
        late = layer == 0
        branch_own = grad_stream.astype(BF16)
        branch_grad = with_partner(branch_own)
        grad_down_b = jnp.sum(branch_own.astype(F32), axis=0)
        if not late:
            reduce_weight(layer, "down", outer_sum(hidden, branch_grad), f"e{layer}")
        pre_grad = (times_transposed(branch_grad, held["down"]) * slope.astype(F32)).astype(BF16)
        two_grad = sum_with_partner(times_transposed(pre_grad, held["up"]))
        grad_up_b = jnp.sum(pre_grad.astype(F32), axis=0)
        middle_back, grad_scale_two, grad_shift_two = norm_backward(
            middle, average_two, inverse_two, scale_two, two_grad
        )
        middle_grad = grad_stream + middle_back
        out_own = middle_grad.astype(BF16)
        out_grad = with_partner(out_own)
        grad_out_b = jnp.sum(out_own.astype(F32), axis=0)
        attended_grad = times_transposed(out_grad, held["out"]).astype(BF16)
        grad_pieces = attended_grad.reshape(tokens, z_count, group).transpose(1, 0, 2)
        grad_pieces = pipeline.advance(xor_order(grad_pieces, z_index), f"b{layer}")
        head_grad = exchange(grad_pieces)
        reduce_weight(layer, "up", outer_sum(normed_two, pre_grad), f"end{layer}")
        if late:
            reduce_weight(layer, "down", outer_sum(hidden, branch_grad), (f"d{layer}", f"e{layer}"))
            reduce_weight(layer, "out", outer_sum(attended, out_grad), f"end{layer}")
        head_grad = pipeline.advance(head_grad, f"c{layer}")
        heads_back = pipeline.advance(attend_back(packed, mixed, head_grad, logs), f"d{layer}")
        if not late:
            reduce_weight(layer, "out", outer_sum(attended, out_grad), f"c{layer - 1}")
        arrived = pipeline.advance(exchange(heads_back), f"e{layer}")
        projected_grad = xor_order(arrived, z_index).transpose(2, 0, 1, 3)
        projected_grad = projected_grad.reshape(tokens, 3 * half_width)
        qkv_points = (f"end{layer}", 1) if late else f"c{layer - 1}"
        reduce_weight(layer, "qkv", outer_sum(normed_one, projected_grad), qkv_points)
        if late:
            projected_grad = pipeline.advance(projected_grad, f"q{layer}")
        one_grad = sum_with_partner(times_transposed(projected_grad, held["qkv"]))
        column_sums = jnp.sum(projected_grad.astype(F32), axis=0).reshape(z_count, 3, group)
        grad_qv_b = jnp.stack([column_sums[:, 0], column_sums[:, 2]])
        stream_back, grad_scale_one, grad_shift_one = norm_backward(
            stream_in, average_one, inverse_one, scale_one, one_grad
        )
        grad_stream = middle_grad + stream_back

        def spread(values, lead):
            values = values.reshape(lead, shards, 1, -1)
            nothing = jnp.zeros_like(values)
            halves = jnp.concatenate(
                [
                    jnp.where(c_index == 0, values, nothing),
                    jnp.where(c_index == 0, nothing, values),
                ],
                axis=2,
            )
            return halves.reshape(shards, -1)

        small = jnp.concatenate(
            [
                member.reshape(shards, -1)
                for member in (
                    grad_scale_one,
                    grad_shift_one,
                    grad_out_b,
                    grad_scale_two,
                    grad_shift_two,
                    grad_down_b,
                    spread(grad_qv_b, 2),
                    spread(grad_up_b, 1),
                )
            ],
            axis=1,
        )
        small = jnp.pad(small.reshape(shards, -1, LANES), ((0, 0), (0, small_rows - offsets[-1] // LANES), (0, 0)))
        reduce_weight(layer, "small", small.reshape(-1, LANES), 1 if late else f"c{layer - 1}")
        grad_stream = pipeline.advance(grad_stream, f"end{layer}")

    pipeline.drain()
    free.drain()
    pipeline.finished.update(pipeline.fresh)
    sums = pipeline.finished
    vector_grads = [sums["small"][:, offsets[place] : offsets[place + 1]] for place in range(8)]
    grad_qkv, grad_out, grad_up, grad_down = sums["qkv"], sums["out"], sums["up"], sums["down"]
    input_grad = grad_stream.reshape(image_count, local_len, width)
    return (
        results,
        input_grad,
        vector_grads[0],
        vector_grads[1],
        grad_qkv,
        vector_grads[6],
        grad_out,
        vector_grads[2],
        vector_grads[3],
        vector_grads[4],
        grad_up,
        vector_grads[7],
        grad_down,
        vector_grads[5],
    )


def solution(mesh):
    seq, shards = mesh.devices.shape
    cores = Mesh(mesh.devices.reshape(seq // 2, 2, shards), ("z", "c", "shard"))
    rows = P("shard", ("z", "c"), None)
    vector = P(None, "shard")
    matrix = P(None, "shard", None)
    parameters = (
        vector,
        vector,
        matrix,
        vector,
        matrix,
        vector,
        vector,
        vector,
        matrix,
        vector,
        matrix,
        vector,
    )
    return jax.shard_map(
        body,
        mesh=cores,
        in_specs=(rows,) + parameters + (rows,),
        out_specs=(rows, rows) + parameters,
        check_vma=False,
    )
```
